32 devices in a mesh: groups: 2 (over x), dom: 16 (over z, y, core).
Axes of the slice: x: 2, y: 2, z: 4, core: 2. Of those that a mesh axis runs over, the one named last changes fastest.
Arguments:
- source: bfloat16 [72, 262144], P(None, ('groups', 'dom')), parts along dimension 1, may hold values from -6 to 6
- tile_weight: bfloat16 [8192, 128, 128], P('dom'), may hold values from -0.0625 to 0.0625
- tile_source: int32 [8192], P('dom'), may hold values from 0 to 127
- tile_slot: int32 [8192], P('dom'), may hold values from 0 to 15
- tile_count: int32 [16], P('dom'), may hold values from 64 to 512, as said below
- dest_block: int32 [256], P('dom'), may hold values from 0 to 63, as said below
- embed_weight: bfloat16 [1152, 1024], replicated, may hold values from -0.1875 to 0.1875
- embed_bias: float32 [1024], replicated, may hold values from -3 to 3
Outputs:
- remapped: bfloat16 [128, 72, 128], P(('groups', 'dom')), parts along dimension 0
- embedded: bfloat16 [1024, 1024], P(('groups', 'dom')), parts along dimension 0
The draws below stay inside these ranges and needn't reach their ends.
There are 2 independent parts, one for each index of `groups`. The reference program is written for one: setup_inputs(seed, part) draws one part's arguments, and reference() takes and returns one part's arrays. A program takes and returns all parts, laid end to end along the dimension named above; an argument that names none is the same for every part. Nothing has to cross between parts.
Inputs may be any that keep to these rules, and one draw needn't show every extreme that they name: `tile_count`: number of live tiles of each device; the later tile slots are unused. Some device has all 512 tiles live. `dest_block`: the owner of target block b is device b // 4. Within one device's 16 entries the blocks are distinct and at most 2 of them belong to any one owner; on every device some owner has exactly 2.
All inputs are finite; a program needn't handle non-finite values.
Results may differ from the reference program's by a relative error of at most 0.0046.
Values may be sent and summed in bfloat16 or wider, within the bound.
A program may use at most 128 MiB of HBM per device.

```python
import jax
import jax.numpy as jnp
from jax import lax

CH = 72
EMB = 1024
BLK = 128
PATCH = 4
CAP = 2
SB_DEV = 64
TB_DEV = 4
TILES_DEV = 512
DSLOT = 16
HALO_B = 32
NSRC = 131072
NTB = 64
NPATCH = 512
N_DOM = 16


def draw_tile_count(key, part):
    levels_table = jnp.array([TILES_DEV, TILES_DEV // 2, TILES_DEV // 4, TILES_DEV // 8], dtype=jnp.int32)
    level_key, busiest_key = jax.random.split(key)
    levels = jax.random.randint(level_key, (N_DOM,), 0, 4)
    counts = levels_table[levels]
    busiest = jax.random.randint(busiest_key, (), 0, N_DOM)
    return jnp.where(jnp.arange(N_DOM) == busiest, TILES_DEV, counts).astype(jnp.int32)


def local_choice(sub_key):
    return jax.random.permutation(sub_key, TB_DEV)[:CAP]


def draw_dest_block(key, part):
    base_key = jax.random.fold_in(key, 11)
    device_keys = jax.random.split(base_key, N_DOM)
    owners_used = DSLOT // CAP

    def for_device(device_key):
        owner_key, local_key, order_key = jax.random.split(device_key, 3)
        owners = jax.random.permutation(owner_key, N_DOM)[:owners_used]
        chosen = jax.vmap(local_choice)(jax.random.split(local_key, owners_used))
        blocks = (owners[:, None] * TB_DEV + chosen).reshape(-1)
        return blocks[jax.random.permutation(order_key, DSLOT)]
    return jax.vmap(for_device)(device_keys).reshape(-1).astype(jnp.int32)


def set_ends(result, rng, least, top_value):
    longest = result.shape.index(max(result.shape))
    spots = []
    for shift in (0, 1):
        where = [jax.random.randint(jax.random.fold_in(rng, axis), (), 0, length) for axis, length in enumerate(result.shape)]
        where[longest] = (where[longest] + shift) % result.shape[longest]
        spots.append(tuple(where))
    return result.at[spots[0]].set(least).at[spots[1]].set(top_value)


def steps_of(stream_key, shape, pieces, least, high):
    loudness = 1.0
    for axis_at, shards_of in pieces:
        draws = jax.random.uniform(jax.random.fold_in(jax.random.fold_in(stream_key, 6), axis_at), (shards_of,), jnp.float32, least / len(pieces), high / len(pieces))
        loudness = loudness * jnp.repeat(jnp.exp(draws), shape[axis_at] // shards_of).reshape((-1,) + (1,) * (len(shape) - 1 - axis_at))
    return loudness


def scatter_about(stream_key, shape, width, reach, shards=(), kind=jnp.bfloat16):
    factor_of = steps_of(stream_key, shape, shards, -0.22, 0.18) if shards else 1.0
    entries = jax.random.normal(stream_key, shape, jnp.float32) * width * factor_of
    return jnp.minimum(jnp.maximum(entries, -reach), reach).astype(kind)


def setup_inputs(seed: int = 0, part: int = 0) -> dict:
    splits = jax.random.split(jax.random.key(seed), 9)
    part_splits = jax.random.split(jax.random.fold_in(splits[8], part), 9)
    return {
        "source": scatter_about(part_splits[0], (CH, NSRC), 1.0, 6.0, ((1, 16),)),
        "tile_weight": scatter_about(splits[1], (N_DOM * TILES_DEV, BLK, BLK), (TILES_DEV * BLK // (2 * TB_DEV)) ** -0.5, 0.0625, ((0, 16),)),
        "tile_source": set_ends(jax.random.randint(splits[2], (N_DOM * TILES_DEV,), 0, 2 * SB_DEV), jax.random.fold_in(splits[2], 1), 0, (2 * SB_DEV) - 1).astype(jnp.int32),
        "tile_slot": set_ends(jax.random.randint(splits[3], (N_DOM * TILES_DEV,), 0, DSLOT), jax.random.fold_in(splits[3], 1), 0, DSLOT - 1).astype(jnp.int32),
        "tile_count": draw_tile_count(jax.random.fold_in(splits[8], 71), part),
        "dest_block": draw_dest_block(jax.random.fold_in(splits[8], 71), part),
        "embed_weight": scatter_about(splits[6], (CH * PATCH * PATCH, EMB), (CH * PATCH * PATCH) ** -0.5, 0.1875),
        "embed_bias": scatter_about(splits[7], (EMB,), 0.5, 3.0, (), jnp.float32),
    }


def reference(source, tile_weight, tile_source, tile_slot, tile_count, dest_block, embed_weight, embed_bias):
    source_total = N_DOM * SB_DEV
    source_blocks = source.reshape(CH, source_total, BLK)

    def add_device(device, totals):
        device = jnp.asarray(device).astype(jnp.int32)
        first_tile = device * TILES_DEV
        offsets = lax.dynamic_slice_in_dim(tile_source, first_tile, TILES_DEV)
        global_ids = ((device * SB_DEV - HALO_B + offsets) % source_total).astype(jnp.int32)
        picked = jnp.take(source_blocks, global_ids, axis=1).astype(jnp.float32)
        weights = lax.dynamic_slice_in_dim(tile_weight, first_tile, TILES_DEV, 0).astype(jnp.float32)
        partial_sums = jnp.einsum("cti,tij->tcj", picked, weights, precision=lax.Precision.HIGHEST)
        active = jnp.arange(TILES_DEV, dtype=jnp.int32) < tile_count[device]
        partial_sums = jnp.where(active[:, None, None], partial_sums, jnp.zeros_like(partial_sums))
        slot_ids = lax.dynamic_slice_in_dim(tile_slot, first_tile, TILES_DEV)
        combined = jax.ops.segment_sum(partial_sums, slot_ids, num_segments=DSLOT)
        targets = lax.dynamic_slice_in_dim(dest_block, device * DSLOT, DSLOT)
        return totals.at[targets].add(combined)

    totals = lax.fori_loop(0, N_DOM, add_device, jnp.zeros((NTB, CH, BLK), jnp.float32))
    remapped = totals.astype(jnp.bfloat16)
    per_block = BLK // (PATCH * PATCH)
    patches = remapped.reshape(NTB, CH, PATCH, per_block, PATCH)
    patches = patches.transpose(0, 3, 1, 2, 4).reshape(NPATCH, CH * PATCH * PATCH)
    embedded = jnp.dot(patches, embed_weight, preferred_element_type=jnp.float32) + embed_bias
    return remapped, embedded.astype(jnp.bfloat16)
```

```python
import functools

import jax
import jax.numpy as jnp
from jax import lax
from jax.experimental import pallas as pl
from jax.experimental.pallas import tpu as pltpu
from jax.sharding import PartitionSpec as P

PATCH = 4
CAP = 2
TB_DEV = 4
GROUP = 16
DEPTH = 4


def tile_steps(order_ref, count_ref, weight_ref, cells_ref, acc_ref, buffer, sems):
    groups = (count_ref[0] + GROUP - 1) // GROUP

    def fetch(group):
        slot = lax.rem(group, DEPTH)
        for i in range(GROUP):
            tile = order_ref[group * GROUP + i] & 0xFFF
            pltpu.make_async_copy(
                weight_ref.at[tile], buffer.at[slot, i], sems.at[slot]
            ).start()

    for group in range(DEPTH):
        @pl.when(group < groups)
        def _():
            fetch(group)

    def step(group, _):
        slot = lax.rem(group, DEPTH)
        pltpu.make_async_copy(
            weight_ref.at[pl.ds(0, GROUP)], buffer.at[slot], sems.at[slot]
        ).wait()
        for first in range(0, GROUP, 4):
            rows, products = [], []
            for i in range(first, first + 4):
                code = order_ref[group * GROUP + i]
                block = (code >> 12) & 0xFF
                rows.append(code >> 20)
                cells = cells_ref[:, pl.ds(pl.multiple_of(block * 128, 128), 128)]
                products.append(
                    jnp.dot(cells, buffer[slot, i], preferred_element_type=jnp.float32)
                )
            for row, product in zip(rows, products):
                acc_ref[row] += product

        @pl.when(group + DEPTH < groups)
        def _():
            fetch(group + DEPTH)

        return 0

    lax.fori_loop(0, groups, step, 0)


def near_kernel(
    order_ref, count_ref, weight_ref, own_ref, fast_ref, acc_ref, cells, buffer, sems, cell_sem
):
    own_cells = own_ref.shape[1]
    copies = [
        pltpu.make_async_copy(own_ref, cells.at[:, pl.ds(0, own_cells)], cell_sem.at[0]),
        pltpu.make_async_copy(
            fast_ref, cells.at[:, pl.ds(own_cells, fast_ref.shape[1])], cell_sem.at[1]
        ),
    ]
    for copy in copies:
        copy.start()
    acc_ref[...] = jnp.zeros_like(acc_ref)
    for copy in copies:
        copy.wait()
    tile_steps(order_ref, count_ref, weight_ref, cells, acc_ref, buffer, sems)


def far_kernel(
    order_ref, count_ref, weight_ref, slow_ref, acc_in_ref, out_ref, acc, buffer, sems, acc_sem
):
    copy = pltpu.make_async_copy(acc_in_ref, acc, acc_sem)
    copy.start()
    copy.wait()
    tile_steps(order_ref, count_ref, weight_ref, slow_ref, acc, buffer, sems)
    rows = out_ref.shape[0]
    out_ref[...] = acc[pl.ds(0, rows)].astype(jnp.bfloat16)


def exchange_kernel(
    peers,
    out_ref,
    label_ref,
    embed_ref,
    bias_ref,
    remapped_ref,
    embedded_ref,
    incoming,
    labels,
    embed,
    padded,
    turned,
    send_sem,
    recv_sem,
    label_send_sem,
    label_recv_sem,
    embed_sem,
):
    me = lax.axis_index("dom")
    channels = out_ref.shape[2]
    barrier = pltpu.get_barrier_semaphore()

    def greet(k, _):
        pl.semaphore_signal(
            barrier,
            inc=1,
            device_id={"dom": lax.rem(me + k, peers)},
            device_id_type=pl.DeviceIdType.MESH,
        )
        return 0

    lax.fori_loop(1, peers, greet, 0)
    embed_copy = pltpu.make_async_copy(embed_ref, embed, embed_sem)
    embed_copy.start()
    pl.semaphore_wait(barrier, peers - 1)

    def copies(k):
        peer = lax.rem(me + k, peers)
        return (
            pltpu.make_async_remote_copy(
                src_ref=label_ref.at[peer],
                dst_ref=labels.at[me],
                send_sem=label_send_sem.at[k],
                recv_sem=label_recv_sem.at[k],
                device_id={"dom": peer},
                device_id_type=pl.DeviceIdType.MESH,
            ),
            pltpu.make_async_remote_copy(
                src_ref=out_ref.at[peer],
                dst_ref=incoming.at[me],
                send_sem=send_sem.at[k],
                recv_sem=recv_sem.at[k],
                device_id={"dom": peer},
                device_id_type=pl.DeviceIdType.MESH,
            ),
        )

    def send(k, _):
        for copy in copies(k):
            copy.start()
        return 0

    lax.fori_loop(1, peers, send, 0)

    def add(totals, rows, names):
        totals = list(totals)
        for r in range(CAP):
            row = rows[r].astype(jnp.float32)
            name = jnp.broadcast_to(names[r : r + 1, :], row.shape)
            for b in range(TB_DEV):
                totals[b] = totals[b] + jnp.where(name == float(b), row, 0.0)
        return tuple(totals)

    zero = jnp.zeros((channels, 128), jnp.float32)
    totals = add((zero,) * TB_DEV, out_ref[me], label_ref[me])

    def receive(k, totals):
        for copy in copies(k):
            copy.wait_recv()
        source = lax.rem(me - k + peers, peers)
        return add(totals, incoming[source], labels[source])

    totals = lax.fori_loop(1, peers, receive, totals)
    padded[...] = jnp.zeros_like(padded)
    for b in range(TB_DEV):
        rounded = totals[b].astype(jnp.bfloat16)
        remapped_ref[b] = rounded
        padded[b, pl.ds(0, channels), :] = rounded.astype(jnp.float32)
    for b in range(TB_DEV):
        turned[pl.ds(b * 128, 128), :] = padded[b].T
    embed_copy.wait()
    per_block = 128 // (PATCH * PATCH)
    stride = PATCH * per_block
    result = jnp.zeros(embedded_ref.shape, jnp.float32)
    for r in range(PATCH):
        for q in range(PATCH):
            parts = [
                turned[pl.ds(b * 128 + r * stride + q, per_block, stride=PATCH), :]
                for b in range(TB_DEV)
            ]
            patch = jnp.concatenate(parts, axis=0).astype(jnp.bfloat16)[:, :channels]
            result = result + jnp.dot(
                patch, embed[r * PATCH + q], preferred_element_type=jnp.float32
            )
    embedded_ref[...] = (result + bias_ref[...]).astype(jnp.bfloat16)

    def finish(k, _):
        for copy in copies(k):
            copy.wait_send()
        return 0

    lax.fori_loop(1, peers, finish, 0)


def local(
    peers,
    source,
    tile_weight,
    tile_source,
    tile_slot,
    tile_count,
    dest_block,
    embed_weight,
    embed_bias,
):
    channels, own_cells = source.shape
    block_size = tile_weight.shape[1]
    own_blocks = own_cells // block_size
    rim_blocks = own_blocks // 2
    rim = rim_blocks * block_size
    tile_total = tile_weight.shape[0]
    slot_total = dest_block.shape[0]
    emb = embed_weight.shape[1]
    rows_out = peers * CAP
    me = lax.axis_index("dom")
    odd = me % 2
    head_start, tail_start = 0, own_cells - rim
    slow_part = lax.dynamic_slice_in_dim(source, jnp.where(odd == 1, tail_start, head_start), rim, 1)
    fast_part = lax.dynamic_slice_in_dim(source, jnp.where(odd == 1, head_start, tail_start), rim, 1)
    slow_pairs = [(i, (i + 1) % peers if i % 2 else (i - 1) % peers) for i in range(peers)]
    fast_pairs = [(i, i + 1 - 2 * (i % 2)) for i in range(peers)]
    fast = lax.ppermute(fast_part, "dom", fast_pairs)
    slow = lax.ppermute(slow_part, "dom", slow_pairs)

    slot_ids = jnp.arange(slot_total, dtype=jnp.int32)
    owners = dest_block // TB_DEV
    earlier = (owners[None, :] == owners[:, None]) & (slot_ids[None, :] < slot_ids[:, None])
    position = owners * CAP + jnp.sum(earlier.astype(jnp.int32), axis=1)
    out_rows = jnp.arange(rows_out, dtype=jnp.int32)
    named = jnp.sum(
        jnp.where(position[None, :] == out_rows[:, None], dest_block[None, :] % TB_DEV + 1, 0), axis=1
    ) - 1
    names = jnp.broadcast_to(
        jnp.pad(named.reshape(peers, CAP), ((0, 0), (0, 8 - CAP)))[:, :, None], (peers, 8, 128)
    ).astype(jnp.float32)

    tile_ids = jnp.arange(tile_total, dtype=jnp.int32)
    row_of = jnp.sum(
        jnp.where(tile_slot[:, None] == slot_ids[None, :], position[None, :], 0), axis=1
    )
    live = tile_ids < tile_count[0]
    left = tile_source < rim_blocks
    right = tile_source >= rim_blocks + own_blocks
    is_far = jnp.where(odd == 1, right, left)
    near = live & ~is_far
    far = live & is_far
    near_block = jnp.where(
        left,
        tile_source + own_blocks,
        jnp.where(right, tile_source - rim_blocks, tile_source - rim_blocks),
    )
    far_block = jnp.where(left, tile_source, tile_source - rim_blocks - own_blocks)
    block = jnp.where(is_far, far_block, near_block)
    code = tile_ids | (block << 12) | (row_of << 20)
    pad_code = rows_out << 20

    def listed(chosen):
        rank = jnp.sum(
            (chosen[None, :] & (tile_ids[None, :] < tile_ids[:, None])).astype(jnp.int32), axis=1
        )
        hit = chosen[None, :] & (rank[None, :] == tile_ids[:, None])
        order = jnp.sum(jnp.where(hit, code[None, :] - pad_code, 0), axis=1) + pad_code
        return order, jnp.sum(chosen.astype(jnp.int32)).reshape(1)

    near_order, near_count = listed(near)
    far_order, far_count = listed(far)

    smem = pl.BlockSpec(memory_space=pltpu.SMEM)
    vmem = pl.BlockSpec(memory_space=pltpu.VMEM)
    hbm = pl.BlockSpec(memory_space=pl.ANY)
    acc_shape = (rows_out + 1, channels, block_size)
    ring = [
        pltpu.VMEM((DEPTH, GROUP, block_size, block_size), jnp.bfloat16),
        pltpu.SemaphoreType.DMA((DEPTH,)),
    ]
    partial = pl.pallas_call(
        near_kernel,
        out_shape=jax.ShapeDtypeStruct(acc_shape, jnp.float32),
        in_specs=[smem, smem, hbm, hbm, hbm],
        out_specs=vmem,
        scratch_shapes=[
            pltpu.VMEM((channels, own_cells + rim), jnp.bfloat16),
            *ring,
            pltpu.SemaphoreType.DMA((2,)),
        ],
        compiler_params=pltpu.CompilerParams(vmem_limit_bytes=32 * 2**20),
        cost_estimate=pl.CostEstimate(
            flops=2 * tile_total * channels * block_size**2,
            bytes_accessed=tile_weight.size * 2,
            transcendentals=0,
        ),
        name="near_tiles",
    )(near_order, near_count, tile_weight, source, fast)
    outgoing = pl.pallas_call(
        far_kernel,
        out_shape=jax.ShapeDtypeStruct((rows_out, channels, block_size), jnp.bfloat16),
        in_specs=[smem, smem, hbm, vmem, hbm],
        out_specs=vmem,
        scratch_shapes=[
            pltpu.VMEM(acc_shape, jnp.float32),
            *ring,
            pltpu.SemaphoreType.DMA,
        ],
        compiler_params=pltpu.CompilerParams(vmem_limit_bytes=32 * 2**20),
        cost_estimate=pl.CostEstimate(
            flops=tile_total * channels * block_size**2,
            bytes_accessed=tile_weight.size,
            transcendentals=0,
        ),
        name="far_tiles",
    )(far_order, far_count, tile_weight, slow, partial)

    per_patch = PATCH * PATCH
    embed_turned = embed_weight.reshape(channels, per_patch, emb).transpose(1, 0, 2)
    patch_rows = TB_DEV * (block_size // per_patch)
    remapped, embedded = pl.pallas_call(
        functools.partial(exchange_kernel, peers),
        out_shape=(
            jax.ShapeDtypeStruct((TB_DEV, channels, block_size), jnp.bfloat16),
            jax.ShapeDtypeStruct((patch_rows, emb), jnp.bfloat16),
        ),
        in_specs=[vmem, vmem, hbm, vmem],
        out_specs=(vmem, vmem),
        scratch_shapes=[
            pltpu.VMEM((peers, CAP, channels, block_size), jnp.bfloat16),
            pltpu.VMEM((peers, 8, 128), jnp.float32),
            pltpu.VMEM((per_patch, channels, emb), jnp.bfloat16),
            pltpu.VMEM((TB_DEV, 128, 128), jnp.float32),
            pltpu.VMEM((TB_DEV * 128, 128), jnp.float32),
            pltpu.SemaphoreType.DMA((peers,)),
            pltpu.SemaphoreType.DMA((peers,)),
            pltpu.SemaphoreType.DMA((peers,)),
            pltpu.SemaphoreType.DMA((peers,)),
            pltpu.SemaphoreType.DMA,
        ],
        compiler_params=pltpu.CompilerParams(
            collective_id=0, has_side_effects=True, vmem_limit_bytes=32 * 2**20
        ),
        name="exchange",
    )(
        outgoing.reshape(peers, CAP, channels, block_size),
        names,
        embed_turned,
        embed_bias.reshape(1, emb),
    )
    return remapped, embedded


def solution(mesh):
    placed = (
        P(None, ("groups", "dom")),
        P("dom", None, None),
        P("dom"),
        P("dom"),
        P("dom"),
        P("dom"),
        P(),
        P(),
    )
    return jax.shard_map(
        functools.partial(local, mesh.shape["dom"]),
        mesh=mesh,
        in_specs=placed,
        out_specs=(P(("groups", "dom"), None, None), P(("groups", "dom"), None)),
        check_vma=False,
    )
```

```python
import functools

import jax
import jax.numpy as jnp
from jax import lax
from jax.experimental import pallas as pl
from jax.experimental.pallas import tpu as pltpu
from jax.sharding import PartitionSpec as P

PATCH = 4
CAP = 2
TB_DEV = 4
QUAD = 4
UNROLL = 4


def load_kernel(after_ref, weight_ref, held_ref, sem):
    copy = pltpu.make_async_copy(weight_ref, held_ref, sem)
    copy.start()
    copy.wait()


def tiles_kernel(order_ref, count_ref, weight_ref, own_ref, fast_ref, slow_ref, out_ref, cells, acc):
    own_blocks = own_ref.shape[1] // 128
    rim_blocks = fast_ref.shape[1] // 128

    def fill(ref, first, blocks):
        def step(i, _):
            for j in range(4):
                b = i * 4 + j
                cells[first + b] = ref[:, pl.ds(pl.multiple_of(b * 128, 128), 128)]
            return 0

        lax.fori_loop(0, blocks // 4, step, 0)

    fill(own_ref, 0, own_blocks)
    fill(fast_ref, own_blocks, rim_blocks)
    fill(slow_ref, own_blocks + rim_blocks, rim_blocks)
    last = cells.shape[0] - 1
    cells[last] = jnp.zeros(cells.shape[1:], cells.dtype)
    acc[...] = jnp.zeros_like(acc)

    def step(group, _):
        rows, products = [], []
        for u in range(UNROLL):
            xs, ws = [], []
            for i in range(QUAD):
                code = order_ref[(group * UNROLL + u) * QUAD + i]
                if i == 0:
                    rows.append(code >> 20)
                xs.append(cells[(code >> 12) & 0xFF])
                ws.append(weight_ref[code & 0xFFF])
            products.append(
                jnp.dot(
                    jnp.concatenate(xs, axis=1),
                    jnp.concatenate(ws, axis=0),
                    preferred_element_type=jnp.float32,
                )
            )
        for row, product in zip(rows, products):
            acc[row] += product
        return 0

    lax.fori_loop(0, count_ref[0], step, 0)
    peers = out_ref.shape[0]

    def store(p, _):
        for r in range(CAP):
            out_ref[p, r] = acc[p * CAP + r].astype(jnp.bfloat16)
        return 0

    lax.fori_loop(0, peers, store, 0)


def exchange_kernel(
    peers,
    out_ref,
    label_ref,
    embed_ref,
    bias_ref,
    remapped_ref,
    embedded_ref,
    incoming,
    labels,
    embed,
    padded,
    turned,
    send_sem,
    recv_sem,
    label_send_sem,
    label_recv_sem,
    embed_sem,
):
    me = lax.axis_index("dom")
    channels = out_ref.shape[2]
    barrier = pltpu.get_barrier_semaphore()

    def greet(k, _):
        pl.semaphore_signal(
            barrier,
            inc=1,
            device_id={"dom": lax.rem(me + k, peers)},
            device_id_type=pl.DeviceIdType.MESH,
        )
        return 0

    lax.fori_loop(1, peers, greet, 0)
    embed_copy = pltpu.make_async_copy(embed_ref, embed, embed_sem)
    embed_copy.start()
    pl.semaphore_wait(barrier, peers - 1)

    def copies(k):
        peer = lax.rem(me + k, peers)
        return (
            pltpu.make_async_remote_copy(
                src_ref=label_ref.at[peer],
                dst_ref=labels.at[me],
                send_sem=label_send_sem.at[k],
                recv_sem=label_recv_sem.at[k],
                device_id={"dom": peer},
                device_id_type=pl.DeviceIdType.MESH,
            ),
            pltpu.make_async_remote_copy(
                src_ref=out_ref.at[peer],
                dst_ref=incoming.at[me],
                send_sem=send_sem.at[k],
                recv_sem=recv_sem.at[k],
                device_id={"dom": peer},
                device_id_type=pl.DeviceIdType.MESH,
            ),
        )

    def send(k, _):
        for copy in copies(k):
            copy.start()
        return 0

    lax.fori_loop(1, peers, send, 0)

    def add(totals, rows, names):
        totals = list(totals)
        for r in range(CAP):
            row = rows[r].astype(jnp.float32)
            name = jnp.broadcast_to(names[r : r + 1, :], row.shape)
            for b in range(TB_DEV):
                totals[b] = totals[b] + jnp.where(name == float(b), row, 0.0)
        return tuple(totals)

    zero = jnp.zeros((channels, 128), jnp.float32)
    totals = add((zero,) * TB_DEV, out_ref[me], label_ref[me])

    def receive(k, totals):
        for copy in copies(k):
            copy.wait_recv()
        source = lax.rem(me - k + peers, peers)
        return add(totals, incoming[source], labels[source])

    totals = lax.fori_loop(1, peers, receive, totals)
    padded[...] = jnp.zeros_like(padded)
    for b in range(TB_DEV):
        rounded = totals[b].astype(jnp.bfloat16)
        remapped_ref[b] = rounded
        padded[b, pl.ds(0, channels), :] = rounded.astype(jnp.float32)
    for b in range(TB_DEV):
        turned[pl.ds(b * 128, 128), :] = padded[b].T
    embed_copy.wait()
    per_block = 128 // (PATCH * PATCH)
    stride = PATCH * per_block
    result = jnp.zeros(embedded_ref.shape, jnp.float32)
    for r in range(PATCH):
        for q in range(PATCH):
            parts = [
                turned[pl.ds(b * 128 + r * stride + q, per_block, stride=PATCH), :]
                for b in range(TB_DEV)
            ]
            patch = jnp.concatenate(parts, axis=0).astype(jnp.bfloat16)[:, :channels]
            result = result + jnp.dot(
                patch, embed[r * PATCH + q], preferred_element_type=jnp.float32
            )
    embedded_ref[...] = (result + bias_ref[...]).astype(jnp.bfloat16)

    def finish(k, _):
        for copy in copies(k):
            copy.wait_send()
        return 0

    lax.fori_loop(1, peers, finish, 0)


def local(
    peers,
    source,
    tile_weight,
    tile_source,
    tile_slot,
    tile_count,
    dest_block,
    embed_weight,
    embed_bias,
):
    channels, own_cells = source.shape
    block_size = tile_weight.shape[1]
    own_blocks = own_cells // block_size
    rim_blocks = own_blocks // 2
    rim = rim_blocks * block_size
    ext_blocks = own_blocks + 2 * rim_blocks
    tile_total = tile_weight.shape[0]
    slot_total = dest_block.shape[0]
    emb = embed_weight.shape[1]
    rows_out = peers * CAP
    me = lax.axis_index("dom")
    odd = me % 2
    head_start, tail_start = 0, own_cells - rim
    slow_part = lax.dynamic_slice_in_dim(source, jnp.where(odd == 1, tail_start, head_start), rim, 1)
    fast_part = lax.dynamic_slice_in_dim(source, jnp.where(odd == 1, head_start, tail_start), rim, 1)
    slow_pairs = [(i, (i + 1) % peers if i % 2 else (i - 1) % peers) for i in range(peers)]
    fast_pairs = [(i, i + 1 - 2 * (i % 2)) for i in range(peers)]
    fast = lax.ppermute(fast_part, "dom", fast_pairs)
    slow = lax.ppermute(slow_part, "dom", slow_pairs)

    slot_ids = jnp.arange(slot_total, dtype=jnp.int32)
    owners = dest_block // TB_DEV
    earlier = (owners[None, :] == owners[:, None]) & (slot_ids[None, :] < slot_ids[:, None])
    position = owners * CAP + jnp.sum(earlier.astype(jnp.int32), axis=1)
    out_rows = jnp.arange(rows_out, dtype=jnp.int32)
    named = jnp.sum(
        jnp.where(position[None, :] == out_rows[:, None], dest_block[None, :] % TB_DEV + 1, 0), axis=1
    ) - 1
    names = jnp.broadcast_to(
        jnp.pad(named.reshape(peers, CAP), ((0, 0), (0, 8 - CAP)))[:, :, None], (peers, 8, 128)
    ).astype(jnp.float32)

    tile_ids = jnp.arange(tile_total, dtype=jnp.int32)
    live = tile_ids < tile_count[0]
    key = jnp.where(live, tile_slot, slot_total)
    rank = jnp.sum(
        ((key[None, :] == key[:, None]) & (tile_ids[None, :] < tile_ids[:, None])).astype(jnp.int32),
        axis=1,
    )
    held = jnp.sum((key[None, :] == slot_ids[:, None]).astype(jnp.int32), axis=1)
    quads = (held + QUAD - 1) // QUAD
    base = jnp.sum(jnp.where(slot_ids[None, :] < slot_ids[:, None], quads[None, :], 0), axis=1) * QUAD
    list_total = -(-(tile_total + (QUAD - 1) * slot_total) // (QUAD * UNROLL)) * QUAD * UNROLL
    table = base + (position << 12)
    entry = jnp.sum(jnp.where(key[:, None] == slot_ids[None, :], table[None, :], 0), axis=1)
    place = jnp.where(live, (entry & 0xFFF) + rank, -1)
    block = jnp.where(
        tile_source < rim_blocks,
        tile_source + own_blocks + jnp.where(odd == 1, 0, rim_blocks),
        tile_source
        - rim_blocks
        + jnp.where((tile_source >= rim_blocks + own_blocks) & (odd == 1), rim_blocks, 0),
    )
    code = tile_ids | (block << 12) | ((entry >> 12) << 20)
    pad_code = (rows_out << 20) | (ext_blocks << 12)
    spots = jnp.arange(list_total, dtype=jnp.int32)
    order = (
        jnp.sum(jnp.where(place[None, :] == spots[:, None], code[None, :] - pad_code, 0), axis=1)
        + pad_code
    )
    steps = ((jnp.sum(quads) + UNROLL - 1) // UNROLL).reshape(1)

    smem = pl.BlockSpec(memory_space=pltpu.SMEM)
    vmem = pl.BlockSpec(memory_space=pltpu.VMEM)
    hbm = pl.BlockSpec(memory_space=pl.ANY)
    weight_held = pl.pallas_call(
        load_kernel,
        out_shape=jax.ShapeDtypeStruct(tile_weight.shape, tile_weight.dtype),
        in_specs=[smem, hbm],
        out_specs=vmem,
        scratch_shapes=[pltpu.SemaphoreType.DMA],
        compiler_params=pltpu.CompilerParams(vmem_limit_bytes=24 * 2**20),
        cost_estimate=pl.CostEstimate(
            flops=0, bytes_accessed=tile_weight.size * 2, transcendentals=0
        ),
        name="load",
    )(held, tile_weight)
    outgoing = pl.pallas_call(
        tiles_kernel,
        out_shape=jax.ShapeDtypeStruct((peers, CAP, channels, block_size), jnp.bfloat16),
        in_specs=[smem, smem, vmem, vmem, vmem, vmem],
        out_specs=vmem,
        scratch_shapes=[
            pltpu.VMEM((ext_blocks + 1, channels, block_size), jnp.bfloat16),
            pltpu.VMEM((rows_out + 1, channels, block_size), jnp.float32),
        ],
        compiler_params=pltpu.CompilerParams(vmem_limit_bytes=32 * 2**20),
        cost_estimate=pl.CostEstimate(
            flops=2 * tile_total * channels * block_size**2,
            bytes_accessed=tile_weight.size * 2,
            transcendentals=0,
        ),
        name="tiles",
    )(order, steps, weight_held, source, fast, slow)

    per_patch = PATCH * PATCH
    embed_turned = embed_weight.reshape(channels, per_patch, emb).transpose(1, 0, 2)
    patch_rows = TB_DEV * (block_size // per_patch)
    remapped, embedded = pl.pallas_call(
        functools.partial(exchange_kernel, peers),
        out_shape=(
            jax.ShapeDtypeStruct((TB_DEV, channels, block_size), jnp.bfloat16),
            jax.ShapeDtypeStruct((patch_rows, emb), jnp.bfloat16),
        ),
        in_specs=[vmem, vmem, hbm, vmem],
        out_specs=(vmem, vmem),
        scratch_shapes=[
            pltpu.VMEM((peers, CAP, channels, block_size), jnp.bfloat16),
            pltpu.VMEM((peers, 8, 128), jnp.float32),
            pltpu.VMEM((per_patch, channels, emb), jnp.bfloat16),
            pltpu.VMEM((TB_DEV, 128, 128), jnp.float32),
            pltpu.VMEM((TB_DEV * 128, 128), jnp.float32),
            pltpu.SemaphoreType.DMA((peers,)),
            pltpu.SemaphoreType.DMA((peers,)),
            pltpu.SemaphoreType.DMA((peers,)),
            pltpu.SemaphoreType.DMA((peers,)),
            pltpu.SemaphoreType.DMA,
        ],
        compiler_params=pltpu.CompilerParams(
            collective_id=0, has_side_effects=True, vmem_limit_bytes=32 * 2**20
        ),
        name="exchange",
    )(
        outgoing,
        names,
        embed_turned,
        embed_bias.reshape(1, emb),
    )
    return remapped, embedded


def solution(mesh):
    placed = (
        P(None, ("groups", "dom")),
        P("dom", None, None),
        P("dom"),
        P("dom"),
        P("dom"),
        P("dom"),
        P(),
        P(),
    )
    return jax.shard_map(
        functools.partial(local, mesh.shape["dom"]),
        mesh=mesh,
        in_specs=placed,
        out_specs=(P(("groups", "dom"), None, None), P(("groups", "dom"), None)),
        check_vma=False,
    )
```

```python
import functools

import jax
import jax.numpy as jnp
from jax import lax
from jax.experimental import pallas as pl
from jax.experimental.pallas import tpu as pltpu
from jax.sharding import PartitionSpec as P

PATCH = 4
CAP = 2
TB_DEV = 4
QUAD = 4
UNROLL = 4


def load_kernel(after_ref, weight_ref, held_ref, sem):
    copy = pltpu.make_async_copy(weight_ref, held_ref, sem)
    copy.start()
    copy.wait()


def tiles_kernel(order_ref, count_ref, weight_ref, own_ref, fast_ref, slow_ref, out_ref, cells, acc):
    own_blocks = own_ref.shape[1] // 128
    rim_blocks = fast_ref.shape[1] // 128

    def fill(ref, first, blocks):
        def step(i, _):
            for j in range(4):
                b = i * 4 + j
                cells[first + b] = ref[:, pl.ds(pl.multiple_of(b * 128, 128), 128)]
            return 0

        lax.fori_loop(0, blocks // 4, step, 0)

    fill(own_ref, 0, own_blocks)
    fill(fast_ref, own_blocks, rim_blocks)
    fill(slow_ref, own_blocks + rim_blocks, rim_blocks)
    last = cells.shape[0] - 1
    cells[last] = jnp.zeros(cells.shape[1:], cells.dtype)
    acc[...] = jnp.zeros_like(acc)

    def step(group, _):
        rows, products = [], []
        for u in range(UNROLL):
            xs, ws = [], []
            for i in range(QUAD):
                code = order_ref[(group * UNROLL + u) * QUAD + i]
                if i == 0:
                    rows.append(code >> 20)
                xs.append(cells[(code >> 12) & 0xFF])
                ws.append(weight_ref[code & 0xFFF])
            products.append(
                jnp.dot(
                    jnp.concatenate(xs, axis=1),
                    jnp.concatenate(ws, axis=0),
                    preferred_element_type=jnp.float32,
                )
            )
        for row, product in zip(rows, products):
            acc[row] += product
        return 0

    lax.fori_loop(0, count_ref[0], step, 0)
    peers = out_ref.shape[0]

    def store(p, _):
        for r in range(CAP):
            out_ref[p, r] = acc[p * CAP + r].astype(jnp.bfloat16)
        return 0

    lax.fori_loop(0, peers, store, 0)


def exchange_kernel(
    peers,
    out_ref,
    label_ref,
    embed_ref,
    bias_ref,
    remapped_ref,
    embedded_ref,
    incoming,
    labels,
    embed,
    padded,
    turned,
    send_sem,
    recv_sem,
    label_send_sem,
    label_recv_sem,
    embed_sem,
):
    me = lax.axis_index("dom")
    channels = out_ref.shape[2]
    barrier = pltpu.get_barrier_semaphore()

    def greet(k, _):
        pl.semaphore_signal(
            barrier,
            inc=1,
            device_id={"dom": lax.rem(me + k, peers)},
            device_id_type=pl.DeviceIdType.MESH,
        )
        return 0

    lax.fori_loop(1, peers, greet, 0)
    embed_copy = pltpu.make_async_copy(embed_ref, embed, embed_sem)
    embed_copy.start()
    pl.semaphore_wait(barrier, peers - 1)

    def copies(k):
        peer = lax.rem(me + k, peers)
        return (
            pltpu.make_async_remote_copy(
                src_ref=label_ref.at[peer],
                dst_ref=labels.at[me],
                send_sem=label_send_sem.at[k],
                recv_sem=label_recv_sem.at[k],
                device_id={"dom": peer},
                device_id_type=pl.DeviceIdType.MESH,
            ),
            pltpu.make_async_remote_copy(
                src_ref=out_ref.at[peer],
                dst_ref=incoming.at[me],
                send_sem=send_sem.at[k],
                recv_sem=recv_sem.at[k],
                device_id={"dom": peer},
                device_id_type=pl.DeviceIdType.MESH,
            ),
        )

    def send(k, _):
        for copy in copies(k):
            copy.start()
        return 0

    lax.fori_loop(1, peers, send, 0)

    def add(totals, rows, names):
        totals = list(totals)
        for r in range(CAP):
            row = rows[r].astype(jnp.float32)
            name = jnp.broadcast_to(names[r : r + 1, :], row.shape)
            for b in range(TB_DEV):
                totals[b] = totals[b] + jnp.where(name == float(b), row, 0.0)
        return tuple(totals)

    zero = jnp.zeros((channels, 128), jnp.float32)
    totals = add((zero,) * TB_DEV, out_ref[me], label_ref[me])

    def receive(k, totals):
        for copy in copies(k):
            copy.wait_recv()
        source = lax.rem(me - k + peers, peers)
        return add(totals, incoming[source], labels[source])

    totals = lax.fori_loop(1, peers, receive, totals)
    padded[...] = jnp.zeros_like(padded)
    for b in range(TB_DEV):
        rounded = totals[b].astype(jnp.bfloat16)
        remapped_ref[b] = rounded
        padded[b, pl.ds(0, channels), :] = rounded.astype(jnp.float32)
    for b in range(TB_DEV):
        turned[pl.ds(b * 128, 128), :] = padded[b].T
    embed_copy.wait()
    per_block = 128 // (PATCH * PATCH)
    stride = PATCH * per_block
    result = jnp.zeros(embedded_ref.shape, jnp.float32)
    for r in range(PATCH):
        for q in range(PATCH):
            parts = [
                turned[pl.ds(b * 128 + r * stride + q, per_block, stride=PATCH), :]
                for b in range(TB_DEV)
            ]
            patch = jnp.concatenate(parts, axis=0).astype(jnp.bfloat16)[:, :channels]
            result = result + jnp.dot(
                patch, embed[r * PATCH + q], preferred_element_type=jnp.float32
            )
    embedded_ref[...] = (result + bias_ref[...]).astype(jnp.bfloat16)

    def finish(k, _):
        for copy in copies(k):
            copy.wait_send()
        return 0

    lax.fori_loop(1, peers, finish, 0)


def local(
    peers,
    source,
    tile_weight,
    tile_source,
    tile_slot,
    tile_count,
    dest_block,
    embed_weight,
    embed_bias,
):
    channels, own_cells = source.shape
    block_size = tile_weight.shape[1]
    own_blocks = own_cells // block_size
    rim_blocks = own_blocks // 2
    rim = rim_blocks * block_size
    ext_blocks = own_blocks + 2 * rim_blocks
    tile_total = tile_weight.shape[0]
    slot_total = dest_block.shape[0]
    emb = embed_weight.shape[1]
    rows_out = peers * CAP
    me = lax.axis_index("dom")
    odd = me % 2
    head_start, tail_start = 0, own_cells - rim
    slow_part = lax.dynamic_slice_in_dim(source, jnp.where(odd == 1, tail_start, head_start), rim, 1)
    fast_part = lax.dynamic_slice_in_dim(source, jnp.where(odd == 1, head_start, tail_start), rim, 1)
    slow_pairs = [(i, (i + 1) % peers if i % 2 else (i - 1) % peers) for i in range(peers)]
    fast_pairs = [(i, i + 1 - 2 * (i % 2)) for i in range(peers)]
    fast = lax.ppermute(fast_part, "dom", fast_pairs)
    slow = lax.ppermute(slow_part, "dom", slow_pairs)

    slot_ids = jnp.arange(slot_total, dtype=jnp.int32)
    owners = dest_block // TB_DEV
    earlier = (owners[None, :] == owners[:, None]) & (slot_ids[None, :] < slot_ids[:, None])
    position = owners * CAP + jnp.sum(earlier.astype(jnp.int32), axis=1)
    out_rows = jnp.arange(rows_out, dtype=jnp.int32)
    named = jnp.sum(
        jnp.where(position[None, :] == out_rows[:, None], dest_block[None, :] % TB_DEV + 1, 0), axis=1
    ) - 1
    names = jnp.broadcast_to(
        jnp.pad(named.reshape(peers, CAP), ((0, 0), (0, 8 - CAP)))[:, :, None], (peers, 8, 128)
    ).astype(jnp.float32)

    tile_ids = jnp.arange(tile_total, dtype=jnp.int32)
    live = tile_ids < tile_count[0]
    key = jnp.where(live, tile_slot, slot_total)
    rank = jnp.sum(
        ((key[None, :] == key[:, None]) & (tile_ids[None, :] < tile_ids[:, None])).astype(jnp.int32),
        axis=1,
    )
    held = jnp.sum((key[None, :] == slot_ids[:, None]).astype(jnp.int32), axis=1)
    quads = (held + QUAD - 1) // QUAD
    base = jnp.sum(jnp.where(slot_ids[None, :] < slot_ids[:, None], quads[None, :], 0), axis=1) * QUAD
    list_total = -(-(tile_total + (QUAD - 1) * slot_total) // (QUAD * UNROLL)) * QUAD * UNROLL
    table = base + (position << 12)
    entry = jnp.sum(jnp.where(key[:, None] == slot_ids[None, :], table[None, :], 0), axis=1)
    place = jnp.where(live, (entry & 0xFFF) + rank, -1)
    block = jnp.where(
        tile_source < rim_blocks,
        tile_source + own_blocks + jnp.where(odd == 1, 0, rim_blocks),
        tile_source
        - rim_blocks
        + jnp.where((tile_source >= rim_blocks + own_blocks) & (odd == 1), rim_blocks, 0),
    )
    code = tile_ids | (block << 12) | ((entry >> 12) << 20)
    pad_code = (rows_out << 20) | (ext_blocks << 12)
    spots = jnp.arange(list_total, dtype=jnp.int32)
    order = (
        jnp.sum(jnp.where(place[None, :] == spots[:, None], code[None, :] - pad_code, 0), axis=1)
        + pad_code
    )
    steps = ((jnp.sum(quads) + UNROLL - 1) // UNROLL).reshape(1)

    smem = pl.BlockSpec(memory_space=pltpu.SMEM)
    vmem = pl.BlockSpec(memory_space=pltpu.VMEM)
    hbm = pl.BlockSpec(memory_space=pl.ANY)
    weight_held = pl.pallas_call(
        load_kernel,
        out_shape=jax.ShapeDtypeStruct(tile_weight.shape, tile_weight.dtype),
        in_specs=[smem, hbm],
        out_specs=vmem,
        scratch_shapes=[pltpu.SemaphoreType.DMA],
        compiler_params=pltpu.CompilerParams(vmem_limit_bytes=24 * 2**20),
        cost_estimate=pl.CostEstimate(
            flops=0, bytes_accessed=tile_weight.size * 2, transcendentals=0
        ),
        name="load",
    )(order, tile_weight)
    outgoing = pl.pallas_call(
        tiles_kernel,
        out_shape=jax.ShapeDtypeStruct((peers, CAP, channels, block_size), jnp.bfloat16),
        in_specs=[smem, smem, vmem, vmem, vmem, vmem],
        out_specs=vmem,
        scratch_shapes=[
            pltpu.VMEM((ext_blocks + 1, channels, block_size), jnp.bfloat16),
            pltpu.VMEM((rows_out + 1, channels, block_size), jnp.float32),
        ],
        compiler_params=pltpu.CompilerParams(vmem_limit_bytes=32 * 2**20),
        cost_estimate=pl.CostEstimate(
            flops=2 * tile_total * channels * block_size**2,
            bytes_accessed=tile_weight.size * 2,
            transcendentals=0,
        ),
        name="tiles",
    )(order, steps, weight_held, source, fast, slow)

    per_patch = PATCH * PATCH
    embed_turned = embed_weight.reshape(channels, per_patch, emb).transpose(1, 0, 2)
    patch_rows = TB_DEV * (block_size // per_patch)
    remapped, embedded = pl.pallas_call(
        functools.partial(exchange_kernel, peers),
        out_shape=(
            jax.ShapeDtypeStruct((TB_DEV, channels, block_size), jnp.bfloat16),
            jax.ShapeDtypeStruct((patch_rows, emb), jnp.bfloat16),
        ),
        in_specs=[vmem, vmem, hbm, vmem],
        out_specs=(vmem, vmem),
        scratch_shapes=[
            pltpu.VMEM((peers, CAP, channels, block_size), jnp.bfloat16),
            pltpu.VMEM((peers, 8, 128), jnp.float32),
            pltpu.VMEM((per_patch, channels, emb), jnp.bfloat16),
            pltpu.VMEM((TB_DEV, 128, 128), jnp.float32),
            pltpu.VMEM((TB_DEV * 128, 128), jnp.float32),
            pltpu.SemaphoreType.DMA((peers,)),
            pltpu.SemaphoreType.DMA((peers,)),
            pltpu.SemaphoreType.DMA((peers,)),
            pltpu.SemaphoreType.DMA((peers,)),
            pltpu.SemaphoreType.DMA,
        ],
        compiler_params=pltpu.CompilerParams(
            collective_id=0, has_side_effects=True, vmem_limit_bytes=32 * 2**20
        ),
        name="exchange",
    )(
        outgoing,
        names,
        embed_turned,
        embed_bias.reshape(1, emb),
    )
    return remapped, embedded


def solution(mesh):
    placed = (
        P(None, ("groups", "dom")),
        P("dom", None, None),
        P("dom"),
        P("dom"),
        P("dom"),
        P("dom"),
        P(),
        P(),
    )
    return jax.shard_map(
        functools.partial(local, mesh.shape["dom"]),
        mesh=mesh,
        in_specs=placed,
        out_specs=(P(("groups", "dom"), None, None), P(("groups", "dom"), None)),
        check_vma=False,
    )
```

```python
import functools

import jax
import jax.numpy as jnp
from jax import lax
from jax.experimental import pallas as pl
from jax.experimental.pallas import tpu as pltpu
from jax.sharding import PartitionSpec as P

PATCH = 4
CAP = 2
TB_DEV = 4
QUAD = 4
UNROLL = 4


def first_tiles(total):
    return total * 3 // 8


def gather_kernel(
    peers,
    after_ref,
    count_ref,
    source_ref,
    cells_ref,
    own,
    fast,
    slow,
    send_sem,
    recv_sem,
    own_sem,
):
    me = lax.axis_index("dom")
    odd = lax.rem(me, 2)
    own_cells, rim = own.shape[1], fast.shape[1]
    own_blocks, rim_blocks = own_cells // 128, rim // 128
    near = me + 1 - 2 * odd
    far = lax.rem(me + 2 * odd - 1 + peers, peers)
    own_copy = pltpu.make_async_copy(source_ref, own, own_sem)
    own_copy.start()
    barrier = pltpu.get_barrier_semaphore()
    for peer in (near, far):
        pl.semaphore_signal(
            barrier, inc=1, device_id={"dom": peer}, device_id_type=pl.DeviceIdType.MESH
        )
    pl.semaphore_wait(barrier, 2)
    far_start = pl.multiple_of(odd * (own_cells - rim), 128)
    near_start = pl.multiple_of((1 - odd) * (own_cells - rim), 128)
    copies = [
        pltpu.make_async_remote_copy(
            src_ref=source_ref.at[:, pl.ds(start, rim)],
            dst_ref=target,
            send_sem=send_sem.at[i],
            recv_sem=recv_sem.at[i],
            device_id={"dom": peer},
            device_id_type=pl.DeviceIdType.MESH,
        )
        for i, (start, target, peer) in enumerate(
            ((far_start, slow, far), (near_start, fast, near))
        )
    ]
    for copy in copies:
        copy.start()

    def fill(ref, first, blocks):
        def step(i, _):
            for j in range(4):
                b = i * 4 + j
                cells_ref[first + b] = ref[:, pl.ds(pl.multiple_of(b * 128, 128), 128)]
            return 0

        lax.fori_loop(0, blocks // 4, step, 0)

    cells_ref[own_blocks + 2 * rim_blocks] = jnp.zeros(cells_ref.shape[1:], cells_ref.dtype)
    own_copy.wait()
    fill(own, 0, own_blocks)
    copies[1].wait_recv()
    fill(fast, own_blocks, rim_blocks)
    copies[0].wait_recv()
    fill(slow, own_blocks + rim_blocks, rim_blocks)
    for copy in copies:
        copy.wait_send()


def tiles_kernel(order_ref, count_ref, weight_ref, cells, out_ref, weights, acc, sems):
    first = first_tiles(weight_ref.shape[0])
    copies = [
        pltpu.make_async_copy(weight_ref.at[part], weights.at[part], sems.at[i])
        for i, part in enumerate((pl.ds(0, first), pl.ds(first, weight_ref.shape[0] - first)))
    ]
    for copy in copies:
        copy.start()
    acc[...] = jnp.zeros_like(acc)

    def step(group, _):
        rows, products = [], []
        for u in range(UNROLL):
            xs, ws = [], []
            for i in range(QUAD):
                code = order_ref[(group * UNROLL + u) * QUAD + i]
                if i == 0:
                    rows.append(code >> 20)
                xs.append(cells[(code >> 12) & 0xFF])
                ws.append(weights[code & 0xFFF])
            products.append(
                jnp.dot(
                    jnp.concatenate(xs, axis=1),
                    jnp.concatenate(ws, axis=0),
                    preferred_element_type=jnp.float32,
                )
            )
        for row, product in zip(rows, products):
            acc[row] += product
        return 0

    copies[0].wait()
    lax.fori_loop(0, count_ref[0], step, 0)
    copies[1].wait()
    lax.fori_loop(count_ref[0], count_ref[1], step, 0)
    peers = out_ref.shape[0]

    def store(p, _):
        for r in range(CAP):
            out_ref[p, r] = acc[p * CAP + r].astype(jnp.bfloat16)
        return 0

    lax.fori_loop(0, peers, store, 0)


def exchange_kernel(
    peers,
    out_ref,
    label_ref,
    embed_ref,
    bias_ref,
    remapped_ref,
    embedded_ref,
    incoming,
    labels,
    embed,
    padded,
    turned,
    send_sem,
    recv_sem,
    label_send_sem,
    label_recv_sem,
    embed_sem,
):
    me = lax.axis_index("dom")
    channels = out_ref.shape[2]
    barrier = pltpu.get_barrier_semaphore()

    def greet(k, _):
        pl.semaphore_signal(
            barrier,
            inc=1,
            device_id={"dom": lax.rem(me + k, peers)},
            device_id_type=pl.DeviceIdType.MESH,
        )
        return 0

    lax.fori_loop(1, peers, greet, 0)
    embed_copy = pltpu.make_async_copy(embed_ref, embed, embed_sem)
    embed_copy.start()
    pl.semaphore_wait(barrier, peers - 1)

    def copies(k):
        peer = lax.rem(me + k, peers)
        return (
            pltpu.make_async_remote_copy(
                src_ref=label_ref.at[peer],
                dst_ref=labels.at[me],
                send_sem=label_send_sem.at[k],
                recv_sem=label_recv_sem.at[k],
                device_id={"dom": peer},
                device_id_type=pl.DeviceIdType.MESH,
            ),
            pltpu.make_async_remote_copy(
                src_ref=out_ref.at[peer],
                dst_ref=incoming.at[me],
                send_sem=send_sem.at[k],
                recv_sem=recv_sem.at[k],
                device_id={"dom": peer},
                device_id_type=pl.DeviceIdType.MESH,
            ),
        )

    def send(k, _):
        for copy in copies(k):
            copy.start()
        return 0

    lax.fori_loop(1, peers, send, 0)

    def add(totals, rows, names):
        totals = list(totals)
        for r in range(CAP):
            row = rows[r].astype(jnp.float32)
            name = jnp.broadcast_to(names[r : r + 1, :], row.shape)
            for b in range(TB_DEV):
                totals[b] = totals[b] + jnp.where(name == float(b), row, 0.0)
        return tuple(totals)

    zero = jnp.zeros((channels, 128), jnp.float32)
    totals = add((zero,) * TB_DEV, out_ref[me], label_ref[me])

    def receive(k, totals):
        for copy in copies(k):
            copy.wait_recv()
        source = lax.rem(me - k + peers, peers)
        return add(totals, incoming[source], labels[source])

    totals = lax.fori_loop(1, peers, receive, totals)
    padded[...] = jnp.zeros_like(padded)
    for b in range(TB_DEV):
        rounded = totals[b].astype(jnp.bfloat16)
        remapped_ref[b] = rounded
        padded[b, pl.ds(0, channels), :] = rounded.astype(jnp.float32)
    for b in range(TB_DEV):
        turned[pl.ds(b * 128, 128), :] = padded[b].T
    embed_copy.wait()
    per_block = 128 // (PATCH * PATCH)
    stride = PATCH * per_block
    result = jnp.zeros(embedded_ref.shape, jnp.float32)
    for r in range(PATCH):
        for q in range(PATCH):
            parts = [
                turned[pl.ds(b * 128 + r * stride + q, per_block, stride=PATCH), :]
                for b in range(TB_DEV)
            ]
            patch = jnp.concatenate(parts, axis=0).astype(jnp.bfloat16)[:, :channels]
            result = result + jnp.dot(
                patch, embed[r * PATCH + q], preferred_element_type=jnp.float32
            )
    embedded_ref[...] = (result + bias_ref[...]).astype(jnp.bfloat16)

    def finish(k, _):
        for copy in copies(k):
            copy.wait_send()
        return 0

    lax.fori_loop(1, peers, finish, 0)


def local(
    peers,
    source,
    tile_weight,
    tile_source,
    tile_slot,
    tile_count,
    dest_block,
    embed_weight,
    embed_bias,
):
    channels, own_cells = source.shape
    block_size = tile_weight.shape[1]
    own_blocks = own_cells // block_size
    rim_blocks = own_blocks // 2
    rim = rim_blocks * block_size
    ext_blocks = own_blocks + 2 * rim_blocks
    tile_total = tile_weight.shape[0]
    slot_total = dest_block.shape[0]
    emb = embed_weight.shape[1]
    rows_out = peers * CAP
    me = lax.axis_index("dom")
    odd = me % 2
    slot_ids = jnp.arange(slot_total, dtype=jnp.int32)
    owners = dest_block // TB_DEV
    earlier = (owners[None, :] == owners[:, None]) & (slot_ids[None, :] < slot_ids[:, None])
    position = owners * CAP + jnp.sum(earlier.astype(jnp.int32), axis=1)
    out_rows = jnp.arange(rows_out, dtype=jnp.int32)
    named = jnp.sum(
        jnp.where(position[None, :] == out_rows[:, None], dest_block[None, :] % TB_DEV + 1, 0), axis=1
    ) - 1
    names = jnp.broadcast_to(
        jnp.pad(named.reshape(peers, CAP), ((0, 0), (0, 8 - CAP)))[:, :, None], (peers, 8, 128)
    ).astype(jnp.float32)

    tile_ids = jnp.arange(tile_total, dtype=jnp.int32)
    live = tile_ids < tile_count[0]
    late = (tile_ids >= first_tiles(tile_total)).astype(jnp.int32)
    key = jnp.where(live, tile_slot + late * slot_total, 2 * slot_total)
    key_ids = jnp.arange(2 * slot_total, dtype=jnp.int32)
    rank = jnp.sum(
        ((key[None, :] == key[:, None]) & (tile_ids[None, :] < tile_ids[:, None])).astype(jnp.int32),
        axis=1,
    )
    held = jnp.sum((key[None, :] == key_ids[:, None]).astype(jnp.int32), axis=1)
    quads = (held + QUAD - 1) // QUAD
    early_steps = (
        jnp.sum(jnp.where(key_ids < slot_total, quads, 0)) + UNROLL - 1
    ) // UNROLL
    before = (key_ids[None, :] < key_ids[:, None]) & (
        (key_ids[None, :] >= slot_total) | (key_ids[:, None] < slot_total)
    )
    base = jnp.sum(jnp.where(before, quads[None, :], 0), axis=1)
    base = (base + jnp.where(key_ids >= slot_total, early_steps * UNROLL, 0)) * QUAD
    unit = QUAD * UNROLL
    list_total = -(-(tile_total + (QUAD - 1) * 2 * slot_total) // unit) * unit + unit
    table = base + (jnp.concatenate([position, position]) << 12)
    entry = jnp.sum(jnp.where(key[:, None] == key_ids[None, :], table[None, :], 0), axis=1)
    place = jnp.where(live, (entry & 0xFFF) + rank, -1)
    block = jnp.where(
        tile_source < rim_blocks,
        tile_source + own_blocks + jnp.where(odd == 1, 0, rim_blocks),
        tile_source
        - rim_blocks
        + jnp.where((tile_source >= rim_blocks + own_blocks) & (odd == 1), rim_blocks, 0),
    )
    code = tile_ids | (block << 12) | ((entry >> 12) << 20)
    pad_code = (rows_out << 20) | (ext_blocks << 12)
    spots = jnp.arange(list_total, dtype=jnp.int32)
    order = (
        jnp.sum(jnp.where(place[None, :] == spots[:, None], code[None, :] - pad_code, 0), axis=1)
        + pad_code
    )
    late_steps = (
        jnp.sum(jnp.where(key_ids >= slot_total, quads, 0)) + UNROLL - 1
    ) // UNROLL
    steps = jnp.stack([early_steps, early_steps + late_steps])

    smem = pl.BlockSpec(memory_space=pltpu.SMEM)
    vmem = pl.BlockSpec(memory_space=pltpu.VMEM)
    hbm = pl.BlockSpec(memory_space=pl.ANY)
    order, steps, names = lax.optimization_barrier((order, steps, names))
    cells = pl.pallas_call(
        functools.partial(gather_kernel, peers),
        out_shape=jax.ShapeDtypeStruct((ext_blocks + 1, channels, block_size), source.dtype),
        in_specs=[smem, smem, hbm],
        out_specs=vmem,
        scratch_shapes=[
            pltpu.VMEM((channels, own_cells), source.dtype),
            pltpu.VMEM((channels, rim), source.dtype),
            pltpu.VMEM((channels, rim), source.dtype),
            pltpu.SemaphoreType.DMA((2,)),
            pltpu.SemaphoreType.DMA((2,)),
            pltpu.SemaphoreType.DMA,
        ],
        compiler_params=pltpu.CompilerParams(
            collective_id=1, has_side_effects=True, vmem_limit_bytes=16 * 2**20
        ),
        name="gather",
    )(order, steps, source)
    outgoing = pl.pallas_call(
        tiles_kernel,
        out_shape=jax.ShapeDtypeStruct((peers, CAP, channels, block_size), jnp.bfloat16),
        in_specs=[smem, smem, hbm, vmem],
        out_specs=vmem,
        scratch_shapes=[
            pltpu.VMEM(tile_weight.shape, tile_weight.dtype),
            pltpu.VMEM((rows_out + 1, channels, block_size), jnp.float32),
            pltpu.SemaphoreType.DMA((2,)),
        ],
        compiler_params=pltpu.CompilerParams(vmem_limit_bytes=48 * 2**20),
        cost_estimate=pl.CostEstimate(
            flops=2 * tile_total * channels * block_size**2,
            bytes_accessed=tile_weight.size * 2,
            transcendentals=0,
        ),
        name="tiles",
    )(order, steps, tile_weight, cells)

    per_patch = PATCH * PATCH
    embed_turned = embed_weight.reshape(channels, per_patch, emb).transpose(1, 0, 2)
    patch_rows = TB_DEV * (block_size // per_patch)
    remapped, embedded = pl.pallas_call(
        functools.partial(exchange_kernel, peers),
        out_shape=(
            jax.ShapeDtypeStruct((TB_DEV, channels, block_size), jnp.bfloat16),
            jax.ShapeDtypeStruct((patch_rows, emb), jnp.bfloat16),
        ),
        in_specs=[vmem, vmem, hbm, vmem],
        out_specs=(vmem, vmem),
        scratch_shapes=[
            pltpu.VMEM((peers, CAP, channels, block_size), jnp.bfloat16),
            pltpu.VMEM((peers, 8, 128), jnp.float32),
            pltpu.VMEM((per_patch, channels, emb), jnp.bfloat16),
            pltpu.VMEM((TB_DEV, 128, 128), jnp.float32),
            pltpu.VMEM((TB_DEV * 128, 128), jnp.float32),
            pltpu.SemaphoreType.DMA((peers,)),
            pltpu.SemaphoreType.DMA((peers,)),
            pltpu.SemaphoreType.DMA((peers,)),
            pltpu.SemaphoreType.DMA((peers,)),
            pltpu.SemaphoreType.DMA,
        ],
        compiler_params=pltpu.CompilerParams(
            collective_id=0, has_side_effects=True, vmem_limit_bytes=32 * 2**20
        ),
        name="exchange",
    )(
        outgoing,
        names,
        embed_turned,
        embed_bias.reshape(1, emb),
    )
    return remapped, embedded


def solution(mesh):
    placed = (
        P(None, ("groups", "dom")),
        P("dom", None, None),
        P("dom"),
        P("dom"),
        P("dom"),
        P("dom"),
        P(),
        P(),
    )
    return jax.shard_map(
        functools.partial(local, mesh.shape["dom"]),
        mesh=mesh,
        in_specs=placed,
        out_specs=(P(("groups", "dom"), None, None), P(("groups", "dom"), None)),
        check_vma=False,
    )
```

```python
import functools

import jax
import jax.numpy as jnp
from jax import lax
from jax.experimental import pallas as pl
from jax.experimental.pallas import tpu as pltpu
from jax.sharding import PartitionSpec as P

PATCH = 4
CAP = 2
TB_DEV = 4
QUAD = 4
UNROLL = 4


def first_tiles(total):
    return total * 3 // 8


def tiles_kernel(
    order_ref,
    count_ref,
    weight_ref,
    own_ref,
    fast_ref,
    slow_ref,
    out_ref,
    cells,
    weights,
    acc,
    sems,
):
    first = first_tiles(weight_ref.shape[0])
    copies = [
        pltpu.make_async_copy(weight_ref.at[part], weights.at[part], sems.at[i])
        for i, part in enumerate((pl.ds(0, first), pl.ds(first, weight_ref.shape[0] - first)))
    ]
    for copy in copies:
        copy.start()
    own_blocks = own_ref.shape[1] // 128
    rim_blocks = fast_ref.shape[1] // 128

    def fill(ref, first, blocks):
        def step(i, _):
            for j in range(4):
                b = i * 4 + j
                cells[first + b] = ref[:, pl.ds(pl.multiple_of(b * 128, 128), 128)]
            return 0

        lax.fori_loop(0, blocks // 4, step, 0)

    fill(own_ref, 0, own_blocks)
    fill(fast_ref, own_blocks, rim_blocks)
    fill(slow_ref, own_blocks + rim_blocks, rim_blocks)
    cells[own_blocks + 2 * rim_blocks] = jnp.zeros(cells.shape[1:], cells.dtype)
    acc[...] = jnp.zeros_like(acc)

    def step(group, _):
        rows, products = [], []
        for u in range(UNROLL):
            xs, ws = [], []
            for i in range(QUAD):
                code = order_ref[(group * UNROLL + u) * QUAD + i]
                if i == 0:
                    rows.append(code >> 20)
                xs.append(cells[(code >> 12) & 0xFF])
                ws.append(weights[code & 0xFFF])
            products.append(
                jnp.dot(
                    jnp.concatenate(xs, axis=1),
                    jnp.concatenate(ws, axis=0),
                    preferred_element_type=jnp.float32,
                )
            )
        for row, product in zip(rows, products):
            acc[row] += product
        return 0

    copies[0].wait()
    lax.fori_loop(0, count_ref[0], step, 0)
    copies[1].wait()
    lax.fori_loop(count_ref[0], count_ref[1], step, 0)
    peers = out_ref.shape[0]

    def store(p, _):
        for r in range(CAP):
            out_ref[p, r] = acc[p * CAP + r].astype(jnp.bfloat16)
        return 0

    lax.fori_loop(0, peers, store, 0)


def exchange_kernel(
    peers,
    out_ref,
    label_ref,
    embed_ref,
    bias_ref,
    remapped_ref,
    embedded_ref,
    incoming,
    labels,
    embed,
    padded,
    turned,
    send_sem,
    recv_sem,
    label_send_sem,
    label_recv_sem,
    embed_sem,
):
    me = lax.axis_index("dom")
    channels = out_ref.shape[2]
    barrier = pltpu.get_barrier_semaphore()

    def greet(k, _):
        pl.semaphore_signal(
            barrier,
            inc=1,
            device_id={"dom": lax.rem(me + k, peers)},
            device_id_type=pl.DeviceIdType.MESH,
        )
        return 0

    lax.fori_loop(1, peers, greet, 0)
    embed_copy = pltpu.make_async_copy(embed_ref, embed, embed_sem)
    embed_copy.start()
    pl.semaphore_wait(barrier, peers - 1)

    def copies(k):
        peer = lax.rem(me + k, peers)
        return (
            pltpu.make_async_remote_copy(
                src_ref=label_ref.at[peer],
                dst_ref=labels.at[me],
                send_sem=label_send_sem.at[k],
                recv_sem=label_recv_sem.at[k],
                device_id={"dom": peer},
                device_id_type=pl.DeviceIdType.MESH,
            ),
            pltpu.make_async_remote_copy(
                src_ref=out_ref.at[peer],
                dst_ref=incoming.at[me],
                send_sem=send_sem.at[k],
                recv_sem=recv_sem.at[k],
                device_id={"dom": peer},
                device_id_type=pl.DeviceIdType.MESH,
            ),
        )

    def send(k, _):
        for copy in copies(k):
            copy.start()
        return 0

    lax.fori_loop(1, peers, send, 0)

    def add(totals, rows, names):
        totals = list(totals)
        for r in range(CAP):
            row = rows[r].astype(jnp.float32)
            name = jnp.broadcast_to(names[r : r + 1, :], row.shape)
            for b in range(TB_DEV):
                totals[b] = totals[b] + jnp.where(name == float(b), row, 0.0)
        return tuple(totals)

    zero = jnp.zeros((channels, 128), jnp.float32)
    totals = add((zero,) * TB_DEV, out_ref[me], label_ref[me])

    def receive(k, totals):
        for copy in copies(k):
            copy.wait_recv()
        source = lax.rem(me - k + peers, peers)
        return add(totals, incoming[source], labels[source])

    totals = lax.fori_loop(1, peers, receive, totals)
    padded[...] = jnp.zeros_like(padded)
    for b in range(TB_DEV):
        rounded = totals[b].astype(jnp.bfloat16)
        remapped_ref[b] = rounded
        padded[b, pl.ds(0, channels), :] = rounded.astype(jnp.float32)
    for b in range(TB_DEV):
        turned[pl.ds(b * 128, 128), :] = padded[b].T
    embed_copy.wait()
    per_block = 128 // (PATCH * PATCH)
    stride = PATCH * per_block
    result = jnp.zeros(embedded_ref.shape, jnp.float32)
    for r in range(PATCH):
        for q in range(PATCH):
            parts = [
                turned[pl.ds(b * 128 + r * stride + q, per_block, stride=PATCH), :]
                for b in range(TB_DEV)
            ]
            patch = jnp.concatenate(parts, axis=0).astype(jnp.bfloat16)[:, :channels]
            result = result + jnp.dot(
                patch, embed[r * PATCH + q], preferred_element_type=jnp.float32
            )
    embedded_ref[...] = (result + bias_ref[...]).astype(jnp.bfloat16)

    def finish(k, _):
        for copy in copies(k):
            copy.wait_send()
        return 0

    lax.fori_loop(1, peers, finish, 0)


def local(
    peers,
    source,
    tile_weight,
    tile_source,
    tile_slot,
    tile_count,
    dest_block,
    embed_weight,
    embed_bias,
):
    channels, own_cells = source.shape
    block_size = tile_weight.shape[1]
    own_blocks = own_cells // block_size
    rim_blocks = own_blocks // 2
    rim = rim_blocks * block_size
    ext_blocks = own_blocks + 2 * rim_blocks
    tile_total = tile_weight.shape[0]
    slot_total = dest_block.shape[0]
    emb = embed_weight.shape[1]
    rows_out = peers * CAP
    me = lax.axis_index("dom")
    odd = me % 2
    head_start, tail_start = 0, own_cells - rim
    slow_part = lax.dynamic_slice_in_dim(source, jnp.where(odd == 1, tail_start, head_start), rim, 1)
    fast_part = lax.dynamic_slice_in_dim(source, jnp.where(odd == 1, head_start, tail_start), rim, 1)
    slow_pairs = [(i, (i + 1) % peers if i % 2 else (i - 1) % peers) for i in range(peers)]
    fast_pairs = [(i, i + 1 - 2 * (i % 2)) for i in range(peers)]
    fast = lax.ppermute(fast_part, "dom", fast_pairs)
    slow = lax.ppermute(slow_part, "dom", slow_pairs)

    slot_ids = jnp.arange(slot_total, dtype=jnp.int32)
    owners = dest_block // TB_DEV
    earlier = (owners[None, :] == owners[:, None]) & (slot_ids[None, :] < slot_ids[:, None])
    position = owners * CAP + jnp.sum(earlier.astype(jnp.int32), axis=1)
    out_rows = jnp.arange(rows_out, dtype=jnp.int32)
    named = jnp.sum(
        jnp.where(position[None, :] == out_rows[:, None], dest_block[None, :] % TB_DEV + 1, 0), axis=1
    ) - 1
    names = jnp.broadcast_to(
        jnp.pad(named.reshape(peers, CAP), ((0, 0), (0, 8 - CAP)))[:, :, None], (peers, 8, 128)
    ).astype(jnp.float32)

    tile_ids = jnp.arange(tile_total, dtype=jnp.int32)
    live = tile_ids < tile_count[0]
    late = (tile_ids >= first_tiles(tile_total)).astype(jnp.int32)
    key = jnp.where(live, tile_slot + late * slot_total, 2 * slot_total)
    key_ids = jnp.arange(2 * slot_total, dtype=jnp.int32)
    rank = jnp.sum(
        ((key[None, :] == key[:, None]) & (tile_ids[None, :] < tile_ids[:, None])).astype(jnp.int32),
        axis=1,
    )
    held = jnp.sum((key[None, :] == key_ids[:, None]).astype(jnp.int32), axis=1)
    quads = (held + QUAD - 1) // QUAD
    early_steps = (
        jnp.sum(jnp.where(key_ids < slot_total, quads, 0)) + UNROLL - 1
    ) // UNROLL
    before = (key_ids[None, :] < key_ids[:, None]) & (
        (key_ids[None, :] >= slot_total) | (key_ids[:, None] < slot_total)
    )
    base = jnp.sum(jnp.where(before, quads[None, :], 0), axis=1)
    base = (base + jnp.where(key_ids >= slot_total, early_steps * UNROLL, 0)) * QUAD
    unit = QUAD * UNROLL
    list_total = -(-(tile_total + (QUAD - 1) * 2 * slot_total) // unit) * unit + unit
    table = base + (jnp.concatenate([position, position]) << 12)
    entry = jnp.sum(jnp.where(key[:, None] == key_ids[None, :], table[None, :], 0), axis=1)
    place = jnp.where(live, (entry & 0xFFF) + rank, -1)
    block = jnp.where(
        tile_source < rim_blocks,
        tile_source + own_blocks + jnp.where(odd == 1, 0, rim_blocks),
        tile_source
        - rim_blocks
        + jnp.where((tile_source >= rim_blocks + own_blocks) & (odd == 1), rim_blocks, 0),
    )
    code = tile_ids | (block << 12) | ((entry >> 12) << 20)
    pad_code = (rows_out << 20) | (ext_blocks << 12)
    spots = jnp.arange(list_total, dtype=jnp.int32)
    order = (
        jnp.sum(jnp.where(place[None, :] == spots[:, None], code[None, :] - pad_code, 0), axis=1)
        + pad_code
    )
    late_steps = (
        jnp.sum(jnp.where(key_ids >= slot_total, quads, 0)) + UNROLL - 1
    ) // UNROLL
    steps = jnp.stack([early_steps, early_steps + late_steps])

    smem = pl.BlockSpec(memory_space=pltpu.SMEM)
    vmem = pl.BlockSpec(memory_space=pltpu.VMEM)
    hbm = pl.BlockSpec(memory_space=pl.ANY)
    outgoing = pl.pallas_call(
        tiles_kernel,
        out_shape=jax.ShapeDtypeStruct((peers, CAP, channels, block_size), jnp.bfloat16),
        in_specs=[smem, smem, hbm, vmem, vmem, vmem],
        out_specs=vmem,
        scratch_shapes=[
            pltpu.VMEM((ext_blocks + 1, channels, block_size), source.dtype),
            pltpu.VMEM(tile_weight.shape, tile_weight.dtype),
            pltpu.VMEM((rows_out + 1, channels, block_size), jnp.float32),
            pltpu.SemaphoreType.DMA((2,)),
        ],
        compiler_params=pltpu.CompilerParams(vmem_limit_bytes=48 * 2**20),
        cost_estimate=pl.CostEstimate(
            flops=2 * tile_total * channels * block_size**2,
            bytes_accessed=tile_weight.size * 2,
            transcendentals=0,
        ),
        name="tiles",
    )(order, steps, tile_weight, source, fast, slow)

    per_patch = PATCH * PATCH
    embed_turned = embed_weight.reshape(channels, per_patch, emb).transpose(1, 0, 2)
    patch_rows = TB_DEV * (block_size // per_patch)
    remapped, embedded = pl.pallas_call(
        functools.partial(exchange_kernel, peers),
        out_shape=(
            jax.ShapeDtypeStruct((TB_DEV, channels, block_size), jnp.bfloat16),
            jax.ShapeDtypeStruct((patch_rows, emb), jnp.bfloat16),
        ),
        in_specs=[vmem, vmem, hbm, vmem],
        out_specs=(vmem, vmem),
        scratch_shapes=[
            pltpu.VMEM((peers, CAP, channels, block_size), jnp.bfloat16),
            pltpu.VMEM((peers, 8, 128), jnp.float32),
            pltpu.VMEM((per_patch, channels, emb), jnp.bfloat16),
            pltpu.VMEM((TB_DEV, 128, 128), jnp.float32),
            pltpu.VMEM((TB_DEV * 128, 128), jnp.float32),
            pltpu.SemaphoreType.DMA((peers,)),
            pltpu.SemaphoreType.DMA((peers,)),
            pltpu.SemaphoreType.DMA((peers,)),
            pltpu.SemaphoreType.DMA((peers,)),
            pltpu.SemaphoreType.DMA,
        ],
        compiler_params=pltpu.CompilerParams(
            collective_id=0, has_side_effects=True, vmem_limit_bytes=32 * 2**20
        ),
        name="exchange",
    )(
        outgoing,
        names,
        embed_turned,
        embed_bias.reshape(1, emb),
    )
    return remapped, embedded


def solution(mesh):
    placed = (
        P(None, ("groups", "dom")),
        P("dom", None, None),
        P("dom"),
        P("dom"),
        P("dom"),
        P("dom"),
        P(),
        P(),
    )
    return jax.shard_map(
        functools.partial(local, mesh.shape["dom"]),
        mesh=mesh,
        in_specs=placed,
        out_specs=(P(("groups", "dom"), None, None), P(("groups", "dom"), None)),
        check_vma=False,
    )
```

```python
import functools

import jax
import jax.numpy as jnp
from jax import lax
from jax.experimental import pallas as pl
from jax.experimental.pallas import tpu as pltpu
from jax.sharding import PartitionSpec as P

PATCH = 4
CAP = 2
TB_DEV = 4
QUAD = 4
UNROLL = 4


def first_tiles(total):
    return total * 3 // 8


def rims_kernel(source_ref, slow_ref, fast_ref, sems):
    odd = lax.rem(lax.axis_index("dom"), 2)
    rim = slow_ref.shape[1]
    rest = source_ref.shape[1] - rim
    copies = [
        pltpu.make_async_copy(
            source_ref.at[:, pl.ds(pl.multiple_of(start, 128), rim)], target, sems.at[i]
        )
        for i, (start, target) in enumerate(
            ((odd * rest, slow_ref), ((1 - odd) * rest, fast_ref))
        )
    ]
    for copy in copies:
        copy.start()
    for copy in copies:
        copy.wait()


def tiles_kernel(
    order_ref,
    count_ref,
    weight_ref,
    own_ref,
    fast_ref,
    slow_ref,
    out_ref,
    cells,
    weights,
    acc,
    sems,
):
    first = first_tiles(weight_ref.shape[0])
    copies = [
        pltpu.make_async_copy(weight_ref.at[part], weights.at[part], sems.at[i])
        for i, part in enumerate((pl.ds(0, first), pl.ds(first, weight_ref.shape[0] - first)))
    ]
    for copy in copies:
        copy.start()
    own_blocks = own_ref.shape[1] // 128
    rim_blocks = fast_ref.shape[1] // 128

    def fill(ref, first, blocks):
        def step(i, _):
            for j in range(4):
                b = i * 4 + j
                cells[first + b] = ref[:, pl.ds(pl.multiple_of(b * 128, 128), 128)]
            return 0

        lax.fori_loop(0, blocks // 4, step, 0)

    fill(own_ref, 0, own_blocks)
    fill(fast_ref, own_blocks, rim_blocks)
    fill(slow_ref, own_blocks + rim_blocks, rim_blocks)
    cells[own_blocks + 2 * rim_blocks] = jnp.zeros(cells.shape[1:], cells.dtype)
    acc[...] = jnp.zeros_like(acc)

    def step(group, _):
        rows, products = [], []
        for u in range(UNROLL):
            xs, ws = [], []
            for i in range(QUAD):
                code = order_ref[(group * UNROLL + u) * QUAD + i]
                if i == 0:
                    rows.append(code >> 20)
                xs.append(cells[(code >> 12) & 0xFF])
                ws.append(weights[code & 0xFFF])
            products.append(
                jnp.dot(
                    jnp.concatenate(xs, axis=1),
                    jnp.concatenate(ws, axis=0),
                    preferred_element_type=jnp.float32,
                )
            )
        for row, product in zip(rows, products):
            acc[row] += product
        return 0

    copies[0].wait()
    lax.fori_loop(0, count_ref[0], step, 0)
    copies[1].wait()
    lax.fori_loop(count_ref[0], count_ref[1], step, 0)
    peers = out_ref.shape[0]

    def store(p, _):
        for r in range(CAP):
            out_ref[p, r] = acc[p * CAP + r].astype(jnp.bfloat16)
        return 0

    lax.fori_loop(0, peers, store, 0)


def exchange_kernel(
    peers,
    out_ref,
    label_ref,
    embed_ref,
    bias_ref,
    remapped_ref,
    embedded_ref,
    incoming,
    labels,
    embed,
    padded,
    turned,
    send_sem,
    recv_sem,
    label_send_sem,
    label_recv_sem,
    embed_sem,
):
    me = lax.axis_index("dom")
    channels = out_ref.shape[2]
    barrier = pltpu.get_barrier_semaphore()

    def greet(k, _):
        pl.semaphore_signal(
            barrier,
            inc=1,
            device_id={"dom": lax.rem(me + k, peers)},
            device_id_type=pl.DeviceIdType.MESH,
        )
        return 0

    lax.fori_loop(1, peers, greet, 0)
    embed_copy = pltpu.make_async_copy(embed_ref, embed, embed_sem)
    embed_copy.start()
    pl.semaphore_wait(barrier, peers - 1)

    def copies(k):
        peer = lax.rem(me + k, peers)
        return (
            pltpu.make_async_remote_copy(
                src_ref=label_ref.at[peer],
                dst_ref=labels.at[me],
                send_sem=label_send_sem.at[k],
                recv_sem=label_recv_sem.at[k],
                device_id={"dom": peer},
                device_id_type=pl.DeviceIdType.MESH,
            ),
            pltpu.make_async_remote_copy(
                src_ref=out_ref.at[peer],
                dst_ref=incoming.at[me],
                send_sem=send_sem.at[k],
                recv_sem=recv_sem.at[k],
                device_id={"dom": peer},
                device_id_type=pl.DeviceIdType.MESH,
            ),
        )

    def send(k, _):
        for copy in copies(k):
            copy.start()
        return 0

    lax.fori_loop(1, peers, send, 0)

    def add(totals, rows, names):
        totals = list(totals)
        for r in range(CAP):
            row = rows[r].astype(jnp.float32)
            name = jnp.broadcast_to(names[r : r + 1, :], row.shape)
            for b in range(TB_DEV):
                totals[b] = totals[b] + jnp.where(name == float(b), row, 0.0)
        return tuple(totals)

    zero = jnp.zeros((channels, 128), jnp.float32)
    totals = add((zero,) * TB_DEV, out_ref[me], label_ref[me])

    def receive(k, totals):
        for copy in copies(k):
            copy.wait_recv()
        source = lax.rem(me - k + peers, peers)
        return add(totals, incoming[source], labels[source])

    totals = lax.fori_loop(1, peers, receive, totals)
    padded[...] = jnp.zeros_like(padded)
    for b in range(TB_DEV):
        rounded = totals[b].astype(jnp.bfloat16)
        remapped_ref[b] = rounded
        padded[b, pl.ds(0, channels), :] = rounded.astype(jnp.float32)
    for b in range(TB_DEV):
        turned[pl.ds(b * 128, 128), :] = padded[b].T
    embed_copy.wait()
    per_block = 128 // (PATCH * PATCH)
    stride = PATCH * per_block
    result = jnp.zeros(embedded_ref.shape, jnp.float32)
    for r in range(PATCH):
        for q in range(PATCH):
            parts = [
                turned[pl.ds(b * 128 + r * stride + q, per_block, stride=PATCH), :]
                for b in range(TB_DEV)
            ]
            patch = jnp.concatenate(parts, axis=0).astype(jnp.bfloat16)[:, :channels]
            result = result + jnp.dot(
                patch, embed[r * PATCH + q], preferred_element_type=jnp.float32
            )
    embedded_ref[...] = (result + bias_ref[...]).astype(jnp.bfloat16)

    def finish(k, _):
        for copy in copies(k):
            copy.wait_send()
        return 0

    lax.fori_loop(1, peers, finish, 0)


def local(
    peers,
    source,
    tile_weight,
    tile_source,
    tile_slot,
    tile_count,
    dest_block,
    embed_weight,
    embed_bias,
):
    channels, own_cells = source.shape
    block_size = tile_weight.shape[1]
    own_blocks = own_cells // block_size
    rim_blocks = own_blocks // 2
    rim = rim_blocks * block_size
    ext_blocks = own_blocks + 2 * rim_blocks
    tile_total = tile_weight.shape[0]
    slot_total = dest_block.shape[0]
    emb = embed_weight.shape[1]
    rows_out = peers * CAP
    me = lax.axis_index("dom")
    odd = me % 2
    rim_shape = jax.ShapeDtypeStruct((channels, rim), source.dtype)
    slow_part, fast_part = pl.pallas_call(
        rims_kernel,
        out_shape=(rim_shape, rim_shape),
        in_specs=[pl.BlockSpec(memory_space=pl.ANY)],
        out_specs=(pl.BlockSpec(memory_space=pl.ANY),) * 2,
        scratch_shapes=[pltpu.SemaphoreType.DMA((2,))],
        compiler_params=pltpu.CompilerParams(vmem_limit_bytes=60 * 2**20),
        name="rims",
    )(source)
    slow_pairs = [(i, (i + 1) % peers if i % 2 else (i - 1) % peers) for i in range(peers)]
    fast_pairs = [(i, i + 1 - 2 * (i % 2)) for i in range(peers)]
    fast = lax.ppermute(fast_part, "dom", fast_pairs)
    slow = lax.ppermute(slow_part, "dom", slow_pairs)

    slot_ids = jnp.arange(slot_total, dtype=jnp.int32)
    owners = dest_block // TB_DEV
    earlier = (owners[None, :] == owners[:, None]) & (slot_ids[None, :] < slot_ids[:, None])
    position = owners * CAP + jnp.sum(earlier.astype(jnp.int32), axis=1)
    out_rows = jnp.arange(rows_out, dtype=jnp.int32)
    named = jnp.sum(
        jnp.where(position[None, :] == out_rows[:, None], dest_block[None, :] % TB_DEV + 1, 0), axis=1
    ) - 1
    names = jnp.broadcast_to(
        jnp.pad(named.reshape(peers, CAP), ((0, 0), (0, 8 - CAP)))[:, :, None], (peers, 8, 128)
    ).astype(jnp.float32)

    tile_ids = jnp.arange(tile_total, dtype=jnp.int32)
    live = tile_ids < tile_count[0]
    late = (tile_ids >= first_tiles(tile_total)).astype(jnp.int32)
    key = jnp.where(live, tile_slot + late * slot_total, 2 * slot_total)
    key_ids = jnp.arange(2 * slot_total, dtype=jnp.int32)
    rank = jnp.sum(
        ((key[None, :] == key[:, None]) & (tile_ids[None, :] < tile_ids[:, None])).astype(jnp.int32),
        axis=1,
    )
    held = jnp.sum((key[None, :] == key_ids[:, None]).astype(jnp.int32), axis=1)
    quads = (held + QUAD - 1) // QUAD
    early_steps = (
        jnp.sum(jnp.where(key_ids < slot_total, quads, 0)) + UNROLL - 1
    ) // UNROLL
    before = (key_ids[None, :] < key_ids[:, None]) & (
        (key_ids[None, :] >= slot_total) | (key_ids[:, None] < slot_total)
    )
    base = jnp.sum(jnp.where(before, quads[None, :], 0), axis=1)
    base = (base + jnp.where(key_ids >= slot_total, early_steps * UNROLL, 0)) * QUAD
    unit = QUAD * UNROLL
    list_total = -(-(tile_total + (QUAD - 1) * 2 * slot_total) // unit) * unit + unit
    table = base + (jnp.concatenate([position, position]) << 12)
    entry = jnp.sum(jnp.where(key[:, None] == key_ids[None, :], table[None, :], 0), axis=1)
    place = jnp.where(live, (entry & 0xFFF) + rank, -1)
    block = jnp.where(
        tile_source < rim_blocks,
        tile_source + own_blocks + jnp.where(odd == 1, 0, rim_blocks),
        tile_source
        - rim_blocks
        + jnp.where((tile_source >= rim_blocks + own_blocks) & (odd == 1), rim_blocks, 0),
    )
    code = tile_ids | (block << 12) | ((entry >> 12) << 20)
    pad_code = (rows_out << 20) | (ext_blocks << 12)
    spots = jnp.arange(list_total, dtype=jnp.int32)
    order = (
        jnp.sum(jnp.where(place[None, :] == spots[:, None], code[None, :] - pad_code, 0), axis=1)
        + pad_code
    )
    late_steps = (
        jnp.sum(jnp.where(key_ids >= slot_total, quads, 0)) + UNROLL - 1
    ) // UNROLL
    steps = jnp.stack([early_steps, early_steps + late_steps])

    smem = pl.BlockSpec(memory_space=pltpu.SMEM)
    vmem = pl.BlockSpec(memory_space=pltpu.VMEM)
    hbm = pl.BlockSpec(memory_space=pl.ANY)
    outgoing = pl.pallas_call(
        tiles_kernel,
        out_shape=jax.ShapeDtypeStruct((peers, CAP, channels, block_size), jnp.bfloat16),
        in_specs=[smem, smem, hbm, vmem, vmem, vmem],
        out_specs=vmem,
        scratch_shapes=[
            pltpu.VMEM((ext_blocks + 1, channels, block_size), source.dtype),
            pltpu.VMEM(tile_weight.shape, tile_weight.dtype),
            pltpu.VMEM((rows_out + 1, channels, block_size), jnp.float32),
            pltpu.SemaphoreType.DMA((2,)),
        ],
        compiler_params=pltpu.CompilerParams(vmem_limit_bytes=48 * 2**20),
        cost_estimate=pl.CostEstimate(
            flops=2 * tile_total * channels * block_size**2,
            bytes_accessed=tile_weight.size * 2,
            transcendentals=0,
        ),
        name="tiles",
    )(order, steps, tile_weight, source, fast, slow)

    per_patch = PATCH * PATCH
    embed_turned = embed_weight.reshape(channels, per_patch, emb).transpose(1, 0, 2)
    patch_rows = TB_DEV * (block_size // per_patch)
    remapped, embedded = pl.pallas_call(
        functools.partial(exchange_kernel, peers),
        out_shape=(
            jax.ShapeDtypeStruct((TB_DEV, channels, block_size), jnp.bfloat16),
            jax.ShapeDtypeStruct((patch_rows, emb), jnp.bfloat16),
        ),
        in_specs=[vmem, vmem, hbm, vmem],
        out_specs=(vmem, vmem),
        scratch_shapes=[
            pltpu.VMEM((peers, CAP, channels, block_size), jnp.bfloat16),
            pltpu.VMEM((peers, 8, 128), jnp.float32),
            pltpu.VMEM((per_patch, channels, emb), jnp.bfloat16),
            pltpu.VMEM((TB_DEV, 128, 128), jnp.float32),
            pltpu.VMEM((TB_DEV * 128, 128), jnp.float32),
            pltpu.SemaphoreType.DMA((peers,)),
            pltpu.SemaphoreType.DMA((peers,)),
            pltpu.SemaphoreType.DMA((peers,)),
            pltpu.SemaphoreType.DMA((peers,)),
            pltpu.SemaphoreType.DMA,
        ],
        compiler_params=pltpu.CompilerParams(
            collective_id=0, has_side_effects=True, vmem_limit_bytes=32 * 2**20
        ),
        name="exchange",
    )(
        outgoing,
        names,
        embed_turned,
        embed_bias.reshape(1, emb),
    )
    return remapped, embedded


def solution(mesh):
    placed = (
        P(None, ("groups", "dom")),
        P("dom", None, None),
        P("dom"),
        P("dom"),
        P("dom"),
        P("dom"),
        P(),
        P(),
    )
    return jax.shard_map(
        functools.partial(local, mesh.shape["dom"]),
        mesh=mesh,
        in_specs=placed,
        out_specs=(P(("groups", "dom"), None, None), P(("groups", "dom"), None)),
        check_vma=False,
    )
```

```python
import functools

import jax
import jax.numpy as jnp
from jax import lax
from jax.experimental import pallas as pl
from jax.experimental.pallas import tpu as pltpu
from jax.sharding import PartitionSpec as P

PATCH = 4
CAP = 2
TB_DEV = 4
QUAD = 4
UNROLL = 4


def first_tiles(total):
    return total * 3 // 8


def rims_kernel(source_ref, slow_ref, fast_ref, sems):
    odd = lax.rem(lax.axis_index("dom"), 2)
    rim = slow_ref.shape[1]
    rest = source_ref.shape[1] - rim
    copies = [
        pltpu.make_async_copy(
            source_ref.at[:, pl.ds(pl.multiple_of(start, 128), rim)], target, sems.at[i]
        )
        for i, (start, target) in enumerate(
            ((odd * rest, slow_ref), ((1 - odd) * rest, fast_ref))
        )
    ]
    for copy in copies:
        copy.start()
    for copy in copies:
        copy.wait()


def tiles_kernel(
    order_ref,
    count_ref,
    weight_ref,
    own_ref,
    fast_ref,
    slow_ref,
    out_ref,
    cells,
    weights,
    acc,
    sems,
):
    first = first_tiles(weight_ref.shape[0])
    copies = [
        pltpu.make_async_copy(weight_ref.at[part], weights.at[part], sems.at[i])
        for i, part in enumerate((pl.ds(0, first), pl.ds(first, weight_ref.shape[0] - first)))
    ]
    for copy in copies:
        copy.start()
    own_blocks = own_ref.shape[1] // 128
    rim_blocks = fast_ref.shape[1] // 128

    def fill(ref, first, blocks):
        def step(i, _):
            for j in range(4):
                b = i * 4 + j
                cells[first + b] = ref[:, pl.ds(pl.multiple_of(b * 128, 128), 128)]
            return 0

        lax.fori_loop(0, blocks // 4, step, 0)

    fill(own_ref, 0, own_blocks)
    fill(fast_ref, own_blocks, rim_blocks)
    fill(slow_ref, own_blocks + rim_blocks, rim_blocks)
    cells[own_blocks + 2 * rim_blocks] = jnp.zeros(cells.shape[1:], cells.dtype)
    acc[...] = jnp.zeros_like(acc)

    def step(group, _):
        rows, products = [], []
        for u in range(UNROLL):
            xs, ws = [], []
            for i in range(QUAD):
                code = order_ref[(group * UNROLL + u) * QUAD + i]
                if i == 0:
                    rows.append(code >> 20)
                xs.append(cells[(code >> 12) & 0xFF])
                ws.append(weights[code & 0xFFF])
            products.append(
                jnp.dot(
                    jnp.concatenate(xs, axis=1),
                    jnp.concatenate(ws, axis=0),
                    preferred_element_type=jnp.float32,
                )
            )
        for row, product in zip(rows, products):
            acc[row] += product
        return 0

    copies[0].wait()
    lax.fori_loop(0, count_ref[0], step, 0)
    copies[1].wait()
    lax.fori_loop(count_ref[0], count_ref[1], step, 0)
    peers = out_ref.shape[0]

    def store(p, _):
        for r in range(CAP):
            out_ref[p, r] = acc[p * CAP + r].astype(jnp.bfloat16)
        return 0

    lax.fori_loop(0, peers, store, 0)


def exchange_kernel(
    peers,
    out_ref,
    label_ref,
    embed_ref,
    bias_ref,
    remapped_ref,
    embedded_ref,
    incoming,
    labels,
    embed,
    padded,
    turned,
    send_sem,
    recv_sem,
    label_send_sem,
    label_recv_sem,
    embed_sem,
):
    me = lax.axis_index("dom")
    channels = out_ref.shape[2]
    barrier = pltpu.get_barrier_semaphore()

    def greet(k, _):
        pl.semaphore_signal(
            barrier,
            inc=1,
            device_id={"dom": lax.rem(me + k, peers)},
            device_id_type=pl.DeviceIdType.MESH,
        )
        return 0

    lax.fori_loop(1, peers, greet, 0)
    embed_copy = pltpu.make_async_copy(embed_ref, embed, embed_sem)
    embed_copy.start()
    pl.semaphore_wait(barrier, peers - 1)

    def copies(k):
        peer = lax.rem(me + k, peers)
        return (
            pltpu.make_async_remote_copy(
                src_ref=label_ref.at[peer],
                dst_ref=labels.at[me],
                send_sem=label_send_sem.at[k],
                recv_sem=label_recv_sem.at[k],
                device_id={"dom": peer},
                device_id_type=pl.DeviceIdType.MESH,
            ),
            pltpu.make_async_remote_copy(
                src_ref=out_ref.at[peer],
                dst_ref=incoming.at[me],
                send_sem=send_sem.at[k],
                recv_sem=recv_sem.at[k],
                device_id={"dom": peer},
                device_id_type=pl.DeviceIdType.MESH,
            ),
        )

    def send(k, _):
        for copy in copies(k):
            copy.start()
        return 0

    lax.fori_loop(1, peers, send, 0)

    def add(totals, rows, names):
        totals = list(totals)
        for r in range(CAP):
            row = rows[r].astype(jnp.float32)
            name = jnp.broadcast_to(names[r : r + 1, :], row.shape)
            for b in range(TB_DEV):
                totals[b] = totals[b] + jnp.where(name == float(b), row, 0.0)
        return tuple(totals)

    zero = jnp.zeros((channels, 128), jnp.float32)
    totals = add((zero,) * TB_DEV, out_ref[me], label_ref[me])

    def receive(k, totals):
        for copy in copies(k):
            copy.wait_recv()
        source = lax.rem(me - k + peers, peers)
        return add(totals, incoming[source], labels[source])

    totals = lax.fori_loop(1, peers, receive, totals)
    padded[...] = jnp.zeros_like(padded)
    for b in range(TB_DEV):
        rounded = totals[b].astype(jnp.bfloat16)
        remapped_ref[b] = rounded
        padded[b, pl.ds(0, channels), :] = rounded.astype(jnp.float32)
    for b in range(TB_DEV):
        turned[pl.ds(b * 128, 128), :] = padded[b].T
    embed_copy.wait()
    per_block = 128 // (PATCH * PATCH)
    stride = PATCH * per_block
    result = jnp.zeros(embedded_ref.shape, jnp.float32)
    for r in range(PATCH):
        for q in range(PATCH):
            parts = [
                turned[pl.ds(b * 128 + r * stride + q, per_block, stride=PATCH), :]
                for b in range(TB_DEV)
            ]
            patch = jnp.concatenate(parts, axis=0).astype(jnp.bfloat16)[:, :channels]
            result = result + jnp.dot(
                patch, embed[r * PATCH + q], preferred_element_type=jnp.float32
            )
    embedded_ref[...] = (result + bias_ref[...]).astype(jnp.bfloat16)

    def finish(k, _):
        for copy in copies(k):
            copy.wait_send()
        return 0

    lax.fori_loop(1, peers, finish, 0)


def local(
    peers,
    source,
    tile_weight,
    tile_source,
    tile_slot,
    tile_count,
    dest_block,
    embed_weight,
    embed_bias,
):
    channels, own_cells = source.shape
    block_size = tile_weight.shape[1]
    own_blocks = own_cells // block_size
    rim_blocks = own_blocks // 2
    rim = rim_blocks * block_size
    ext_blocks = own_blocks + 2 * rim_blocks
    tile_total = tile_weight.shape[0]
    slot_total = dest_block.shape[0]
    emb = embed_weight.shape[1]
    rows_out = peers * CAP
    me = lax.axis_index("dom")
    odd = me % 2
    rim_shape = jax.ShapeDtypeStruct((channels, rim), source.dtype)
    slow_part, fast_part = pl.pallas_call(
        rims_kernel,
        out_shape=(rim_shape, rim_shape),
        in_specs=[pl.BlockSpec(memory_space=pl.ANY)],
        out_specs=(pl.BlockSpec(memory_space=pltpu.VMEM),) * 2,
        scratch_shapes=[pltpu.SemaphoreType.DMA((2,))],
        compiler_params=pltpu.CompilerParams(vmem_limit_bytes=60 * 2**20),
        name="rims",
    )(source)
    slow_pairs = [(i, (i + 1) % peers if i % 2 else (i - 1) % peers) for i in range(peers)]
    fast_pairs = [(i, i + 1 - 2 * (i % 2)) for i in range(peers)]
    fast = lax.ppermute(fast_part, "dom", fast_pairs)
    slow = lax.ppermute(slow_part, "dom", slow_pairs)

    slot_ids = jnp.arange(slot_total, dtype=jnp.int32)
    owners = dest_block // TB_DEV
    earlier = (owners[None, :] == owners[:, None]) & (slot_ids[None, :] < slot_ids[:, None])
    position = owners * CAP + jnp.sum(earlier.astype(jnp.int32), axis=1)
    out_rows = jnp.arange(rows_out, dtype=jnp.int32)
    named = jnp.sum(
        jnp.where(position[None, :] == out_rows[:, None], dest_block[None, :] % TB_DEV + 1, 0), axis=1
    ) - 1
    names = jnp.broadcast_to(
        jnp.pad(named.reshape(peers, CAP), ((0, 0), (0, 8 - CAP)))[:, :, None], (peers, 8, 128)
    ).astype(jnp.float32)

    tile_ids = jnp.arange(tile_total, dtype=jnp.int32)
    live = tile_ids < tile_count[0]
    late = (tile_ids >= first_tiles(tile_total)).astype(jnp.int32)
    key = jnp.where(live, tile_slot + late * slot_total, 2 * slot_total)
    key_ids = jnp.arange(2 * slot_total, dtype=jnp.int32)
    rank = jnp.sum(
        ((key[None, :] == key[:, None]) & (tile_ids[None, :] < tile_ids[:, None])).astype(jnp.int32),
        axis=1,
    )
    held = jnp.sum((key[None, :] == key_ids[:, None]).astype(jnp.int32), axis=1)
    quads = (held + QUAD - 1) // QUAD
    early_steps = (
        jnp.sum(jnp.where(key_ids < slot_total, quads, 0)) + UNROLL - 1
    ) // UNROLL
    before = (key_ids[None, :] < key_ids[:, None]) & (
        (key_ids[None, :] >= slot_total) | (key_ids[:, None] < slot_total)
    )
    base = jnp.sum(jnp.where(before, quads[None, :], 0), axis=1)
    base = (base + jnp.where(key_ids >= slot_total, early_steps * UNROLL, 0)) * QUAD
    unit = QUAD * UNROLL
    list_total = -(-(tile_total + (QUAD - 1) * 2 * slot_total) // unit) * unit + unit
    table = base + (jnp.concatenate([position, position]) << 12)
    entry = jnp.sum(jnp.where(key[:, None] == key_ids[None, :], table[None, :], 0), axis=1)
    place = jnp.where(live, (entry & 0xFFF) + rank, -1)
    block = jnp.where(
        tile_source < rim_blocks,
        tile_source + own_blocks + jnp.where(odd == 1, 0, rim_blocks),
        tile_source
        - rim_blocks
        + jnp.where((tile_source >= rim_blocks + own_blocks) & (odd == 1), rim_blocks, 0),
    )
    code = tile_ids | (block << 12) | ((entry >> 12) << 20)
    pad_code = (rows_out << 20) | (ext_blocks << 12)
    spots = jnp.arange(list_total, dtype=jnp.int32)
    order = (
        jnp.sum(jnp.where(place[None, :] == spots[:, None], code[None, :] - pad_code, 0), axis=1)
        + pad_code
    )
    late_steps = (
        jnp.sum(jnp.where(key_ids >= slot_total, quads, 0)) + UNROLL - 1
    ) // UNROLL
    steps = jnp.stack([early_steps, early_steps + late_steps])

    smem = pl.BlockSpec(memory_space=pltpu.SMEM)
    vmem = pl.BlockSpec(memory_space=pltpu.VMEM)
    hbm = pl.BlockSpec(memory_space=pl.ANY)
    outgoing = pl.pallas_call(
        tiles_kernel,
        out_shape=jax.ShapeDtypeStruct((peers, CAP, channels, block_size), jnp.bfloat16),
        in_specs=[smem, smem, hbm, vmem, vmem, vmem],
        out_specs=vmem,
        scratch_shapes=[
            pltpu.VMEM((ext_blocks + 1, channels, block_size), source.dtype),
            pltpu.VMEM(tile_weight.shape, tile_weight.dtype),
            pltpu.VMEM((rows_out + 1, channels, block_size), jnp.float32),
            pltpu.SemaphoreType.DMA((2,)),
        ],
        compiler_params=pltpu.CompilerParams(vmem_limit_bytes=48 * 2**20),
        cost_estimate=pl.CostEstimate(
            flops=2 * tile_total * channels * block_size**2,
            bytes_accessed=tile_weight.size * 2,
            transcendentals=0,
        ),
        name="tiles",
    )(order, steps, tile_weight, source, fast, slow)

    per_patch = PATCH * PATCH
    embed_turned = embed_weight.reshape(channels, per_patch, emb).transpose(1, 0, 2)
    patch_rows = TB_DEV * (block_size // per_patch)
    remapped, embedded = pl.pallas_call(
        functools.partial(exchange_kernel, peers),
        out_shape=(
            jax.ShapeDtypeStruct((TB_DEV, channels, block_size), jnp.bfloat16),
            jax.ShapeDtypeStruct((patch_rows, emb), jnp.bfloat16),
        ),
        in_specs=[vmem, vmem, hbm, vmem],
        out_specs=(vmem, vmem),
        scratch_shapes=[
            pltpu.VMEM((peers, CAP, channels, block_size), jnp.bfloat16),
            pltpu.VMEM((peers, 8, 128), jnp.float32),
            pltpu.VMEM((per_patch, channels, emb), jnp.bfloat16),
            pltpu.VMEM((TB_DEV, 128, 128), jnp.float32),
            pltpu.VMEM((TB_DEV * 128, 128), jnp.float32),
            pltpu.SemaphoreType.DMA((peers,)),
            pltpu.SemaphoreType.DMA((peers,)),
            pltpu.SemaphoreType.DMA((peers,)),
            pltpu.SemaphoreType.DMA((peers,)),
            pltpu.SemaphoreType.DMA,
        ],
        compiler_params=pltpu.CompilerParams(
            collective_id=0, has_side_effects=True, vmem_limit_bytes=32 * 2**20
        ),
        name="exchange",
    )(
        outgoing,
        names,
        embed_turned,
        embed_bias.reshape(1, emb),
    )
    return remapped, embedded


def solution(mesh):
    placed = (
        P(None, ("groups", "dom")),
        P("dom", None, None),
        P("dom"),
        P("dom"),
        P("dom"),
        P("dom"),
        P(),
        P(),
    )
    return jax.shard_map(
        functools.partial(local, mesh.shape["dom"]),
        mesh=mesh,
        in_specs=placed,
        out_specs=(P(("groups", "dom"), None, None), P(("groups", "dom"), None)),
        check_vma=False,
    )
```
